256 devices in a mesh: slab: 32 (over y_hi, z, core), coil: 8 (over x, y_lo).
Axes of the slice: x: 4, y: 4 (y_hi: 2, y_lo: 2; y = y_hi * 2 + y_lo), z: 8, core: 2. Of those that a mesh axis runs over, the one named last changes fastest.
Arguments:
- image: float32 [2, 128, 128, 256], P(None, 'slab'), may hold values from -6 to 6
- sensitivity: float32 [2, 8, 128, 128, 256], P(None, 'coil', 'slab'), may hold values from -2 to 2
- kspace: float32 [2, 8, 128, 128, 256], P(None, 'coil', None, 'slab'), may hold values from -3 to 3
- sampled: int32 [128, 128], P(None, 'slab'), may hold values 0 or 1
- w_in: bfloat16 [27, 16, 2], replicated, may hold values from -0.875 to 0.875
- w_mid: bfloat16 [27, 16, 16], replicated, may hold values from -0.3125 to 0.3125
- w_out: bfloat16 [27, 2, 16], replicated, may hold values from -0.3125 to 0.3125
Outputs:
- refined: float32 [2, 128, 128, 256], P(None, 'slab', 'coil')
- residual: float32 [2, 8, 128, 128, 256], P(None, 'coil', None, 'slab')
The draws below stay inside these ranges and needn't reach their ends.
All inputs are finite; a program needn't handle non-finite values. No bound on the sum of `sampled` on one device may be relied on, other than what follows from the above.
Results may differ from the reference program's by a relative error of at most 0.0023.
Values may be sent and summed in bfloat16 or wider, within the bound.
A program may use at most 64 MiB of HBM per device.

```python
import jax
import jax.numpy as jnp
from jax import lax

NX = 256
NY = 128
NZ = 128
FEAT = 16
GRAD_STEPS = 2
COILS = 8


def set_ends(drawn, own_key, smallest, top_value):
    longest = drawn.shape.index(max(drawn.shape))
    spots = []
    for shift in (0, 1):
        where = [jax.random.randint(jax.random.fold_in(own_key, axis), (), 0, length) for axis, length in enumerate(drawn.shape)]
        where[longest] = (where[longest] + shift) % drawn.shape[longest]
        spots.append(tuple(where))
    return drawn.at[spots[0]].set(smallest).at[spots[1]].set(top_value)


def block_scale(own_key, shape, shards, smallest, high):
    def one(position, parts):
        steps = jax.random.uniform(jax.random.fold_in(jax.random.fold_in(own_key, 6), position), (parts,), jnp.float32, smallest / len(shards), high / len(shards))
        return jnp.repeat(jnp.exp(steps), shape[position] // parts).reshape((-1,) + (1,) * (len(shape) - position - 1))

    loudness = one(*shards[0])
    for cut in shards[1:]:
        loudness = loudness * one(*cut)
    return loudness


def gaussian(own_key, dims, width, limit, shards=(), dtype=jnp.bfloat16):
    entries = jax.random.normal(own_key, dims, jnp.float32) * width
    if len(shards) > 0:
        entries = block_scale(own_key, dims, shards, -0.22, 0.18) * entries
    return jnp.clip(entries, min=-limit, max=limit).astype(dtype)


def setup_inputs(seed: int = 0) -> dict:
    seeds = jax.random.split(jax.random.key(seed), 8)
    return {
        "image": gaussian(seeds[0], (2, NZ, NY, NX), 1.0, 6.0, ((1, 32),), jnp.float32),
        "sensitivity": gaussian(seeds[1], (2, COILS, NZ, NY, NX), COILS ** -0.5, 2.0, ((1, 8), (2, 32)), jnp.float32),
        "kspace": gaussian(seeds[2], (2, COILS, NZ, NY, NX), 0.5, 3.0, ((1, 8), (3, 32)), jnp.float32),
        "sampled": set_ends((jax.random.randint(seeds[3], (NZ, NY), 0, 5) < 2).astype(jnp.int32), jax.random.fold_in(seeds[3], 1), 0, 1),
        "w_in": gaussian(seeds[4], (27, FEAT, 2), 54 ** -0.5, 0.875),
        "w_mid": gaussian(seeds[5], (27, FEAT, FEAT), (27 * FEAT) ** -0.5, 0.3125),
        "w_out": gaussian(seeds[6], (27, 2, FEAT), (27 * FEAT) ** -0.5, 0.3125),
    }


step_size = 0.5


def conv_layer(values, weight):
    count_out = weight.shape[1]
    count_in = weight.shape[2]
    kernel = weight.astype(jnp.float32).reshape(3, 3, 3, count_out, count_in).transpose(3, 4, 0, 1, 2)
    result = lax.conv_general_dilated(values.astype(jnp.float32)[None], kernel, (1, 1, 1), ((1, 1), (1, 1), (1, 1)), dimension_numbers=("NCDHW", "OIDHW", "NCDHW"), precision=lax.Precision.HIGHEST)
    return result[0]


def reference(image, sensitivity, kspace, sampled, w_in, w_mid, w_out):
    current = lax.complex(image[0], image[1])
    coil_maps = lax.complex(sensitivity[0], sensitivity[1])
    measured = lax.complex(kspace[0], kspace[1])
    weight = sampled.astype(jnp.float32)[:, :, None]

    def normal(estimate):
        def one_coil(summed, pair):
            coil_map, data = pair
            spectrum = jnp.fft.fftn(coil_map * estimate, norm="ortho")
            misfit = weight * (spectrum - data)
            back = jnp.conj(coil_map) * jnp.fft.ifftn(misfit, norm="ortho")
            return summed + back, misfit
        return lax.scan(one_coil, jnp.zeros_like(estimate), (coil_maps, measured))

    misfit = None
    for repeat in range(GRAD_STEPS):
        gradient, misfit = normal(current)
        current = current - step_size * gradient
    start = jnp.stack([jnp.real(current), jnp.imag(current)])
    hidden = jax.nn.relu(conv_layer(start.astype(jnp.bfloat16), w_in)).astype(jnp.bfloat16)
    hidden = jax.nn.relu(conv_layer(hidden, w_mid)).astype(jnp.bfloat16)
    refined = start + conv_layer(hidden, w_out)
    residual = jnp.stack([jnp.real(misfit), jnp.imag(misfit)])
    return refined, residual
```

```python
import functools
import math

import jax
import jax.numpy as jnp
import ml_dtypes
import numpy as np
from jax import lax
from jax.experimental import pallas as pl
from jax.experimental.pallas import tpu as pltpu
from jax.sharding import PartitionSpec as P

NX = 256
NY = 128
NZ = 128

step_size = 0.5
SENS_CODE = 16383.0
IMAGE_CODE = 5461.0
DATA_CODE = 3970.0
MESH = pl.DeviceIdType.MESH


def halves(matrix):
    high = matrix.astype(ml_dtypes.bfloat16)
    low = (matrix - high.astype(np.float64)).astype(ml_dtypes.bfloat16)
    return high, low


def blocks(length, inverse):
    positions = np.arange(length)
    angles = (positions[:, None] * positions[None, :] % length) * (2.0 * math.pi / length)
    cosines = np.cos(angles) / math.sqrt(length)
    sines = np.sin(angles) / math.sqrt(length)
    if inverse:
        sines = -sines
    return np.block([[cosines, sines], [-sines, cosines]])


def mixed_rows(matrix):
    return matrix.reshape(2, 32, 4, -1).transpose(1, 0, 2, 3).reshape(256, -1)


def constants():
    forward = blocks(128, False)
    backward = blocks(128, True)
    made = []
    for matrix in (
        mixed_rows(forward.T).T,
        mixed_rows(forward),
        mixed_rows(backward.T).T,
        mixed_rows(backward),
        blocks(256, True),
    ):
        made.extend(halves(matrix))
    return made


def product(pair, data):
    high = data.astype(jnp.bfloat16)
    low = (data - high.astype(jnp.float32)).astype(jnp.bfloat16)
    first, second = (pair[0][...], pair[1][...])
    dot = functools.partial(jnp.dot, preferred_element_type=jnp.float32)
    return dot(first, high) + (dot(first, low) + dot(second, high))


def product_nt(pair, data):
    high = data.astype(jnp.bfloat16)
    low = (data - high.astype(jnp.float32)).astype(jnp.bfloat16)
    first, second = (pair[0][...], pair[1][...])

    def dot(a, b):
        return lax.dot_general(a, b, (((1,), (1,)), ((), ())), preferred_element_type=jnp.float32)

    return dot(first, high) + (dot(first, low) + dot(second, high))


def regrouped(x):
    parts = []
    for k in range(2):
        lanes = slice(128 * k, 128 * k + 128)
        parts.append(jnp.concatenate([x[:128, lanes], x[128:, lanes]], axis=1))
    return jnp.concatenate(parts, axis=0)


def swapped(x):
    return pltpu.roll(x.reshape(32, 8, 128), 4, 1).reshape(256, 128)


def coded(x, scale):
    return jnp.round(x * scale).astype(jnp.int32).astype(jnp.int16)


def companded(x):
    size = jnp.sqrt(jnp.abs(x)) * DATA_CODE
    return jnp.round(jnp.where(x < 0, -size, size)).astype(jnp.int32).astype(jnp.int16)


def decoded(x):
    return x.astype(jnp.int32).astype(jnp.float32)


def gradient_kernel(
    image, sens, kspace, sampled, g1f_h, g1f_l, g2f_h, g2f_l, g1i_h, g1i_l, g2i_h, g2i_l, x_h, x_l,
    current_out, residual_out,
    s_msg, s_rcv, i_msg, i_rcv, y_msg, y_rcv, a_msg, a_rcv, c_msg, c_rcv,
    tmp, sens_a, sens_b, spec, cur, send_sem, recv_sem,
):
    slab = lax.axis_index("slab")
    coil = lax.axis_index("coil")
    me = slab * 8 + coil
    g1f, g2f, g1i, g2i, gx = ((g1f_h, g1f_l), (g2f_h, g2f_l), (g1i_h, g1i_l), (g2i_h, g2i_l), (x_h, x_l))

    def device(p):
        return p // 8, lax.rem(p, 8)

    barrier = pltpu.get_barrier_semaphore()

    def greet(k, _):
        s, c = device(lax.rem(me + k, 256))
        pl.semaphore_signal(barrier, inc=1, device_id={"slab": s, "coil": c}, device_id_type=MESH)
        return 0

    lax.fori_loop(1, 256, greet, 0)

    def send_all(msg, rcv, which):
        def one(k, _):
            s, c = device(lax.rem(me + k, 256))
            pltpu.make_async_remote_copy(
                msg.at[s, c], rcv.at[slab, coil], send_sem.at[which], recv_sem.at[which],
                device_id={"slab": s, "coil": c}, device_id_type=MESH,
            ).start()
            return 0

        lax.fori_loop(1, 256, one, 0)
        rcv[slab, coil] = msg[slab, coil]

    for ri in range(2):
        for z in range(4):
            tmp[:, :, ri * 4 + z, :] = sens[ri, 0, z].T.reshape(32, 8, 128)
    s_msg[...] = coded(tmp[...], SENS_CODE)
    for ri in range(2):
        for z in range(4):
            tmp[:, :, ri * 4 + z, :] = image[ri, z].T.reshape(32, 8, 128)
    rows = lax.broadcasted_iota(jnp.int32, (8, 4), 0)
    columns = lax.broadcasted_iota(jnp.int32, (8, 4), 1)
    pick = (lax.rem(rows, 4) == columns).astype(jnp.float32)
    mask = lax.dot_general(
        pick, sampled[...].astype(jnp.float32), (((1,), (1,)), ((), ())), preferred_element_type=jnp.float32
    )
    own = coded(tmp[:, coil], IMAGE_CODE)
    i_msg[:, 0] = own
    i_msg[:, 1] = jnp.broadcast_to(coded(mask, 1.0)[None], (32, 8, 128))

    pl.semaphore_wait(barrier, 255)

    def send_image(k, _):
        s = lax.rem(slab + k, 32)
        pltpu.make_async_remote_copy(
            i_msg.at[s], i_rcv.at[slab], send_sem.at[0], recv_sem.at[0],
            device_id={"slab": s, "coil": coil}, device_id_type=MESH,
        ).start()
        return 0

    lax.fori_loop(1, 32, send_image, 0)
    i_rcv[slab] = i_msg[slab]
    send_all(s_msg, s_rcv, 1)

    stacked = jnp.concatenate(
        [jnp.concatenate([kspace[0, 0, :, k, :], kspace[1, 0, :, k, :]], axis=1) for k in range(4)], axis=0
    )
    hybrid = product_nt(gx, stacked)
    for ri in range(2):
        for k in range(4):
            tmp[:, :, ri * 4 + k, :] = hybrid[256 * ri : 256 * ri + 256, 128 * k : 128 * k + 128].reshape(32, 8, 128)
    y_msg[...] = companded(tmp[...])
    send_all(y_msg, y_rcv, 2)

    def arrived(flat, which, count):
        part = flat.at[pl.ds(0, count)]
        pltpu.make_async_copy(part, part, recv_sem.at[which]).wait()

    def left(flat, which, count):
        part = flat.at[pl.ds(0, count)]
        pltpu.make_async_copy(part, part, send_sem.at[which]).wait()

    arrived(i_rcv, 0, 31)
    arrived(s_rcv.reshape(256, 8, 128), 1, 255)
    cur[...] = decoded(i_rcv[:, 0]).reshape(256, 128) * (1.0 / IMAGE_CODE)

    lower = lax.broadcasted_iota(jnp.int32, (256, 128), 0) % 8 < 4

    def unpack(c, _):
        both = decoded(s_rcv[:, c]).reshape(256, 128) * (1.0 / SENS_CODE)
        other = swapped(both)
        sens_a[c] = jnp.where(lower, both, other)
        sens_b[c] = jnp.where(lower, -other, both)
        return 0

    lax.fori_loop(0, 8, unpack, 0)

    def forward(p, now, turned):
        c = 2 * p
        v = jnp.concatenate(
            [sens_a[c] * now + sens_b[c] * turned, sens_a[c + 1] * now + sens_b[c + 1] * turned], axis=1
        )
        return product_nt(g2f, regrouped(product(g1f, v)))

    def backward(p, found, weight):
        c = 2 * p
        res = []
        for k in range(2):
            code = decoded(y_rcv[:, c + k]).reshape(256, 128)
            data = code * jnp.abs(code) * (1.0 / DATA_CODE**2)
            res.append(weight * (found[:, 128 * k : 128 * k + 128] - data))
        b = product_nt(g2i, regrouped(product(g1i, jnp.concatenate(res, axis=1))))
        total = None
        for k in range(2):
            part = b[:, 128 * k : 128 * k + 128]
            term = sens_a[c + k] * part - sens_b[c + k] * swapped(part)
            total = term if total is None else total + term
        return total

    now = cur[...]
    turned = swapped(now)

    def ahead(p, _):
        spec[p] = forward(p, now, turned)
        return 0

    lax.fori_loop(0, 4, ahead, 0)
    arrived(y_rcv.reshape(256, 8, 128), 2, 255)
    weight = decoded(i_rcv[:, 1]).reshape(256, 128)
    grad = lax.fori_loop(0, 4, lambda p, g: g + backward(p, spec[p], weight), jnp.zeros((256, 128), jnp.float32))
    now_1 = now - step_size * grad
    turned_1 = swapped(now_1)

    def again(p, g):
        found = forward(p, now_1, turned_1)
        for k in range(2):
            a_msg[:, 2 * p + k] = found[:, 128 * k : 128 * k + 128].reshape(32, 8, 128).astype(jnp.bfloat16)
        return g + backward(p, found, weight)

    grad = lax.fori_loop(0, 4, again, jnp.zeros((256, 128), jnp.float32))
    cur[...] = now_1 - step_size * grad

    lane = lax.broadcasted_iota(jnp.int32, (32, 128), 1) // 16
    picked = [cur[pl.ds(r, 32, stride=8), :] for r in range(8)]
    for c in range(8):
        packed = None
        for r in range(8):
            shift = 16 * ((r - c) % 8)
            moved = pltpu.roll(picked[r], shift, 1) if shift else picked[r]
            packed = moved if packed is None else jnp.where(lane == r, moved, packed)
        c_msg[:, c, 0, :] = packed
    send_all(c_msg, c_rcv, 4)
    send_all(a_msg, a_rcv, 3)

    arrived(c_rcv.reshape(256, 1, 128), 4, 255)
    current_out[...] = c_rcv[:, :, 0, :].reshape(256, 128).T

    arrived(a_rcv.reshape(256, 8, 128), 3, 255)
    tmp[...] = a_rcv[...].astype(jnp.float32)
    keep = sampled[...].astype(jnp.float32)
    for k in range(4):
        parts = [tmp[:, :, 4 * ri + k, :].reshape(256, 128).T.astype(jnp.bfloat16) for ri in range(2)]
        found = jnp.concatenate(parts, axis=1)
        found = jnp.dot(found, x_h[...], preferred_element_type=jnp.float32) + jnp.dot(
            found, x_l[...], preferred_element_type=jnp.float32
        )
        here = keep[:, k : k + 1]
        residual_out[0, 0, :, k, :] = here * (found[:, :256] - kspace[0, 0, :, k, :])
        residual_out[1, 0, :, k, :] = here * (found[:, 256:] - kspace[1, 0, :, k, :])
    left(i_msg, 0, 31)
    left(s_msg.reshape(256, 8, 128), 1, 255)
    left(y_msg.reshape(256, 8, 128), 2, 255)
    left(a_msg.reshape(256, 8, 128), 3, 255)
    left(c_msg.reshape(256, 1, 128), 4, 255)


def gradient_steps(image, sensitivity, kspace, sampled):
    whole = pl.BlockSpec(memory_space=pltpu.VMEM)
    tables = [jnp.asarray(m) for m in constants()]
    small = [pltpu.VMEM((32, 8, 8, 128), jnp.int16) for _ in range(2)]
    return pl.pallas_call(
        gradient_kernel,
        out_shape=(
            jax.ShapeDtypeStruct((128, 256), jnp.float32),
            jax.ShapeDtypeStruct((2, 1, 128, 4, 256), jnp.float32),
        ),
        in_specs=[whole] * (4 + len(tables)),
        out_specs=(whole, whole),
        scratch_shapes=small
        + [pltpu.VMEM((32, 2, 8, 128), jnp.int16) for _ in range(2)]
        + small
        + [pltpu.VMEM((32, 8, 8, 128), jnp.bfloat16) for _ in range(2)]
        + [pltpu.VMEM((32, 8, 1, 128), jnp.float32) for _ in range(2)]
        + [
            pltpu.VMEM((32, 8, 8, 128), jnp.float32),
            pltpu.VMEM((8, 256, 128), jnp.float32),
            pltpu.VMEM((8, 256, 128), jnp.float32),
            pltpu.VMEM((4, 256, 256), jnp.float32),
            pltpu.VMEM((256, 128), jnp.float32),
            pltpu.SemaphoreType.DMA((5,)),
            pltpu.SemaphoreType.DMA((5,)),
        ],
        compiler_params=pltpu.CompilerParams(
            collective_id=0, has_side_effects=True, vmem_limit_bytes=48 * 1024 * 1024
        ),
        name="gradient_steps",
    )(image, sensitivity, kspace, sampled, *tables)


def padded_2(x, sides, width):
    for axis, dim in sides:
        size, length = (lax.axis_size(axis), x.shape[dim])
        up = [(i, (i + 1) % size) for i in range(size - 1)]
        down = [(j, i) for i, j in up]
        last = lax.slice_in_dim(x, length - width, length, axis=dim)
        leading = lax.slice_in_dim(x, 0, width, axis=dim)
        before = lax.ppermute(last, axis, up)
        after = lax.ppermute(leading, axis, down)
        x = jnp.concatenate([before, x, after], axis=dim)
    return x


def conv_layer(padded, weight):
    extent_z = padded.shape[1] - 2
    extent_y = padded.shape[2] - 2
    width = padded.shape[3]
    shifted_left = jnp.pad(padded[:, :, :, : width - 1], ((0, 0), (0, 0), (0, 0), (1, 0)))
    shifted_right = jnp.pad(padded[:, :, :, 1:], ((0, 0), (0, 0), (0, 0), (0, 1)))
    stacked = jnp.concatenate([shifted_left, padded, shifted_right], axis=0)
    summed = None
    for offset_z in range(3):
        for offset_y in range(3):
            tap_block = jnp.concatenate(
                [weight[9 * offset_z + 3 * offset_y + offset_x] for offset_x in range(3)], axis=1
            )
            window = stacked[:, offset_z : offset_z + extent_z, offset_y : offset_y + extent_y, :]
            partial_value = jnp.einsum(
                "oi,izyx->ozyx", tap_block, window, preferred_element_type=jnp.float32
            )
            summed = partial_value if summed is None else summed + partial_value
    return summed


def shards(image, sensitivity, kspace, sampled, w_in, w_mid, w_out):
    slab_depth = image.shape[1]
    row_count = image.shape[2] // lax.axis_size("coil")
    current, residual = gradient_steps(image, sensitivity, kspace, sampled)
    current = current.reshape(2, slab_depth, row_count, NX)
    row_start = lax.axis_index("coil") * row_count
    start = current.astype(jnp.bfloat16)
    grown = padded_2(start, (("slab", 1), ("coil", 2)), 3)
    base_z = lax.axis_index("slab") * slab_depth

    def inside(margin):
        cells_z = base_z - margin + jnp.arange(slab_depth + 2 * margin, dtype=jnp.int32)
        cells_y = row_start - margin + jnp.arange(row_count + 2 * margin, dtype=jnp.int32)
        valid_z = ((cells_z >= 0) & (cells_z < NZ)).astype(jnp.float32)
        valid_y = ((cells_y >= 0) & (cells_y < NY)).astype(jnp.float32)
        return (valid_z[:, None] * valid_y[None, :])[None, :, :, None]

    hidden = (jax.nn.relu(conv_layer(grown, w_in)) * inside(2)).astype(jnp.bfloat16)
    hidden = (jax.nn.relu(conv_layer(hidden, w_mid)) * inside(1)).astype(jnp.bfloat16)
    result = conv_layer(hidden, w_out)
    refined = current + result
    return (refined, residual)


def solution(mesh):
    placed = (
        P(None, "slab", None, None),
        P(None, "coil", "slab", None, None),
        P(None, "coil", None, "slab", None),
        P(None, "slab"),
        P(),
        P(),
        P(),
    )
    return jax.shard_map(
        shards,
        mesh=mesh,
        in_specs=placed,
        out_specs=(P(None, "slab", "coil", None), P(None, "coil", None, "slab", None)),
        check_vma=False,
    )
```

```python
import functools
import math

import jax
import jax.numpy as jnp
import ml_dtypes
import numpy as np
from jax import lax
from jax.experimental import pallas as pl
from jax.experimental.pallas import tpu as pltpu
from jax.sharding import PartitionSpec as P

NX = 256
NY = 128
NZ = 128

step_size = 0.5
SENS_CODE = 16383.0
IMAGE_CODE = 5461.0
DATA_CODE = 3970.0
MESH = pl.DeviceIdType.MESH


def halves(matrix):
    high = matrix.astype(ml_dtypes.bfloat16)
    low = (matrix - high.astype(np.float64)).astype(ml_dtypes.bfloat16)
    return high, low


def blocks(length, inverse):
    positions = np.arange(length)
    angles = (positions[:, None] * positions[None, :] % length) * (2.0 * math.pi / length)
    cosines = np.cos(angles) / math.sqrt(length)
    sines = np.sin(angles) / math.sqrt(length)
    if inverse:
        sines = -sines
    return np.block([[cosines, sines], [-sines, cosines]])


def mixed_rows(matrix):
    return matrix.reshape(2, 32, 4, -1).transpose(1, 0, 2, 3).reshape(256, -1)


def constants():
    forward = blocks(128, False)
    backward = blocks(128, True)
    made = []
    for matrix in (
        mixed_rows(forward.T).T,
        mixed_rows(forward),
        mixed_rows(backward.T).T,
        mixed_rows(backward),
        blocks(256, True),
    ):
        made.extend(halves(matrix))
    return made


def product(pair, data):
    high = data.astype(jnp.bfloat16)
    low = (data - high.astype(jnp.float32)).astype(jnp.bfloat16)
    first, second = (pair[0][...], pair[1][...])
    dot = functools.partial(jnp.dot, preferred_element_type=jnp.float32)
    return dot(first, high) + (dot(first, low) + dot(second, high))


def product_nt(pair, data):
    high = data.astype(jnp.bfloat16)
    low = (data - high.astype(jnp.float32)).astype(jnp.bfloat16)
    first, second = (pair[0][...], pair[1][...])

    def dot(a, b):
        return lax.dot_general(a, b, (((1,), (1,)), ((), ())), preferred_element_type=jnp.float32)

    return dot(first, high) + (dot(first, low) + dot(second, high))


def regrouped(x):
    parts = []
    for k in range(2):
        lanes = slice(128 * k, 128 * k + 128)
        parts.append(jnp.concatenate([x[:128, lanes], x[128:, lanes]], axis=1))
    return jnp.concatenate(parts, axis=0)


def swapped(x):
    return pltpu.roll(x.reshape(32, 8, 128), 4, 1).reshape(256, 128)


def coded(x, scale):
    return jnp.round(x * scale).astype(jnp.int32).astype(jnp.int16)


def companded(x):
    size = jnp.sqrt(jnp.abs(x)) * DATA_CODE
    return jnp.round(jnp.where(x < 0, -size, size)).astype(jnp.int32).astype(jnp.int16)


def decoded(x):
    return x.astype(jnp.int32).astype(jnp.float32)


def padded_rows(ref, z):
    return ref[pl.ds(z, 3)].reshape(432, 256)


def unrolled_kernel(*refs):
    count = len(OPERANDS)
    held = refs[count + 2 : 2 * count + 2]
    load_sem = refs[2 * count + 2]
    loads = [pltpu.make_async_copy(refs[k], held[k], load_sem.at[k]) for k in range(count)]
    for load in loads:
        load.start()
    image, sens, kspace, sampled, base_1, weight_2, base_3 = held[:7]
    g1f_h, g1f_l, g2f_h, g2f_l, g1i_h, g1i_l, g2i_h, g2i_l, x_h, x_l = held[7:]
    refined_out, residual_out = refs[count : count + 2]
    (
        s_msg, s_rcv, i_msg, i_rcv, y_msg, y_rcv, a_msg, a_rcv, c_msg, c_rcv,
        tmp, sens_a, sens_b, spec, cur,
        zh_msg, zh_rcv, yh_msg, yh_rcv, ch_msg, ch_rcv,
        block, grown, wide_0, wide_1, wide_2, toeplitz_1, toeplitz_3, matrix_1, matrix_3,
        send_sem, recv_sem, halo_send, halo_recv,
    ) = refs[2 * count + 3 :]
    slab = lax.axis_index("slab")
    coil = lax.axis_index("coil")
    me = slab * 8 + coil
    g1f, g2f, g1i, g2i, gx = ((g1f_h, g1f_l), (g2f_h, g2f_l), (g1i_h, g1i_l), (g2i_h, g2i_l), (x_h, x_l))

    def device(p):
        return p // 8, lax.rem(p, 8)

    barrier = pltpu.get_barrier_semaphore()

    def greet(k, _):
        s, c = device(lax.rem(me + k, 256))
        pl.semaphore_signal(barrier, inc=1, device_id={"slab": s, "coil": c}, device_id_type=MESH)
        return 0

    lax.fori_loop(1, 256, greet, 0)

    def send_all(msg, rcv, which):
        def one(k, _):
            s, c = device(lax.rem(me + k, 256))
            pltpu.make_async_remote_copy(
                msg.at[s, c], rcv.at[slab, coil], send_sem.at[which], recv_sem.at[which],
                device_id={"slab": s, "coil": c}, device_id_type=MESH,
            ).start()
            return 0

        lax.fori_loop(1, 256, one, 0)
        rcv[slab, coil] = msg[slab, coil]

    loads[1].wait()
    for ri in range(2):
        for z in range(4):
            tmp[:, :, ri * 4 + z, :] = sens[ri, 0, z].T.reshape(32, 8, 128)
    s_msg[...] = coded(tmp[...], SENS_CODE)
    loads[0].wait()
    loads[3].wait()
    for ri in range(2):
        for z in range(4):
            tmp[:, :, ri * 4 + z, :] = image[ri, z].T.reshape(32, 8, 128)
    rows = lax.broadcasted_iota(jnp.int32, (8, 4), 0)
    columns = lax.broadcasted_iota(jnp.int32, (8, 4), 1)
    pick = (lax.rem(rows, 4) == columns).astype(jnp.float32)
    mask = lax.dot_general(
        pick, sampled[...].astype(jnp.float32), (((1,), (1,)), ((), ())), preferred_element_type=jnp.float32
    )
    own = coded(tmp[:, coil], IMAGE_CODE)
    i_msg[:, 0] = own
    i_msg[:, 1] = jnp.broadcast_to(coded(mask, 1.0)[None], (32, 8, 128))

    for number in (2, *range(4, count)):
        loads[number].wait()
    for o in range(16):
        spread = jnp.broadcast_to(base_1[o : o + 1, :], (24, 512))
        turned = pltpu.roll(spread, 0, 1, stride=1, stride_axis=0)
        for part in range(4):
            toeplitz_1[part, pl.ds(o, 20, stride=16), :] = turned[:20, 128 * part : 128 * part + 128]
    for part in range(4):
        matrix_1[:, 128 * part : 128 * part + 128] = toeplitz_1[part].astype(jnp.bfloat16)
    for y in range(16):
        turned = pltpu.roll(base_3[...], 48 * y, 1) if y else base_3[...]
        for part in range(7):
            toeplitz_3[part, :, y, :] = turned[:, 128 * part : 128 * part + 128]
    for dz in range(3):
        for ri in range(2):
            for part in range(7):
                matrix_3[dz, 16 * ri : 16 * ri + 16, 128 * part : 128 * part + 128] = toeplitz_3[
                    part, 2 * dz + ri
                ].astype(jnp.bfloat16)
    grown[...] = jnp.zeros((10, 2, 24, 256), jnp.float32)

    pl.semaphore_wait(barrier, 255)

    def send_image(k, _):
        s = lax.rem(slab + k, 32)
        pltpu.make_async_remote_copy(
            i_msg.at[s], i_rcv.at[slab], send_sem.at[0], recv_sem.at[0],
            device_id={"slab": s, "coil": coil}, device_id_type=MESH,
        ).start()
        return 0

    lax.fori_loop(1, 32, send_image, 0)
    i_rcv[slab] = i_msg[slab]
    send_all(s_msg, s_rcv, 1)

    stacked = jnp.concatenate(
        [jnp.concatenate([kspace[0, 0, :, k, :], kspace[1, 0, :, k, :]], axis=1) for k in range(4)], axis=0
    )
    hybrid = product_nt(gx, stacked)
    for ri in range(2):
        for k in range(4):
            tmp[:, :, ri * 4 + k, :] = hybrid[256 * ri : 256 * ri + 256, 128 * k : 128 * k + 128].reshape(32, 8, 128)
    y_msg[...] = companded(tmp[...])
    send_all(y_msg, y_rcv, 2)

    def arrived(flat, which, count):
        part = flat.at[pl.ds(0, count)]
        pltpu.make_async_copy(part, part, recv_sem.at[which]).wait()

    def left(flat, which, count):
        part = flat.at[pl.ds(0, count)]
        pltpu.make_async_copy(part, part, send_sem.at[which]).wait()

    arrived(i_rcv, 0, 31)
    arrived(s_rcv.reshape(256, 8, 128), 1, 255)
    cur[...] = decoded(i_rcv[:, 0]).reshape(256, 128) * (1.0 / IMAGE_CODE)

    lower = lax.broadcasted_iota(jnp.int32, (256, 128), 0) % 8 < 4

    def unpack(c, _):
        both = decoded(s_rcv[:, c]).reshape(256, 128) * (1.0 / SENS_CODE)
        other = swapped(both)
        sens_a[c] = jnp.where(lower, both, other)
        sens_b[c] = jnp.where(lower, -other, both)
        return 0

    lax.fori_loop(0, 8, unpack, 0)

    def forward(p, now, turned):
        c = 2 * p
        v = jnp.concatenate(
            [sens_a[c] * now + sens_b[c] * turned, sens_a[c + 1] * now + sens_b[c + 1] * turned], axis=1
        )
        return product_nt(g2f, regrouped(product(g1f, v)))

    def backward(p, found, weight):
        c = 2 * p
        res = []
        for k in range(2):
            code = decoded(y_rcv[:, c + k]).reshape(256, 128)
            data = code * jnp.abs(code) * (1.0 / DATA_CODE**2)
            res.append(weight * (found[:, 128 * k : 128 * k + 128] - data))
        b = product_nt(g2i, regrouped(product(g1i, jnp.concatenate(res, axis=1))))
        total = None
        for k in range(2):
            part = b[:, 128 * k : 128 * k + 128]
            term = sens_a[c + k] * part - sens_b[c + k] * swapped(part)
            total = term if total is None else total + term
        return total

    now = cur[...]
    turned = swapped(now)

    def ahead(p, _):
        spec[p] = forward(p, now, turned)
        return 0

    lax.fori_loop(0, 4, ahead, 0)
    arrived(y_rcv.reshape(256, 8, 128), 2, 255)
    weight = decoded(i_rcv[:, 1]).reshape(256, 128)
    grad = lax.fori_loop(0, 4, lambda p, g: g + backward(p, spec[p], weight), jnp.zeros((256, 128), jnp.float32))
    now_1 = now - step_size * grad
    turned_1 = swapped(now_1)

    def again(p, g):
        found = forward(p, now_1, turned_1)
        for k in range(2):
            a_msg[:, 2 * p + k] = found[:, 128 * k : 128 * k + 128].reshape(32, 8, 128).astype(jnp.bfloat16)
        return g + backward(p, found, weight)

    grad = lax.fori_loop(0, 4, again, jnp.zeros((256, 128), jnp.float32))
    cur[...] = now_1 - step_size * grad

    lane = lax.broadcasted_iota(jnp.int32, (32, 128), 1) // 16
    picked = [cur[pl.ds(r, 32, stride=8), :] for r in range(8)]
    for c in range(8):
        packed = None
        for r in range(8):
            shift = 16 * ((r - c) % 8)
            moved = pltpu.roll(picked[r], shift, 1) if shift else picked[r]
            packed = moved if packed is None else jnp.where(lane == r, moved, packed)
        c_msg[:, c, 0, :] = packed
    send_all(c_msg, c_rcv, 4)
    arrived(c_rcv.reshape(256, 1, 128), 4, 255)
    block[...] = c_rcv[:, :, 0, :].reshape(256, 128).T

    starts = [[block[64 * ri + 16 * z : 64 * ri + 16 * z + 16, :] for ri in range(2)] for z in range(4)]
    for z in range(4):
        for ri in range(2):
            first = starts[z][ri][:8].astype(jnp.bfloat16)
            last = starts[z][ri][8:].astype(jnp.bfloat16)
            yh_msg[0, z, ri] = first
            yh_msg[1, z, ri] = last
            for side in range(2):
                if 0 <= z - side < 3:
                    zh_msg[side, z - side, ri] = starts[z][ri].astype(jnp.bfloat16)
                    ch_msg[side, 0, z - side, ri] = first
                    ch_msg[side, 1, z - side, ri] = last

    halos = []
    for side in range(2):
        s = lax.rem(slab + (31 if side == 0 else 1), 32)
        c = lax.rem(coil + (7 if side == 0 else 1), 8)
        halos.append((zh_msg.at[side], zh_rcv.at[1 - side], s, coil))
        halos.append((yh_msg.at[side], yh_rcv.at[1 - side], slab, c))
        for other in range(2):
            c = lax.rem(coil + (7 if other == 0 else 1), 8)
            halos.append((ch_msg.at[side, other], ch_rcv.at[1 - side, 1 - other], s, c))
    halos = [
        pltpu.make_async_remote_copy(
            src, dst, halo_send.at[k], halo_recv.at[k], device_id={"slab": s, "coil": c}, device_id_type=MESH
        )
        for k, (src, dst, s, c) in enumerate(halos)
    ]
    for halo in halos:
        halo.start()
    send_all(a_msg, a_rcv, 3)
    for halo in halos:
        halo.wait()

    lane_x = lax.broadcasted_iota(jnp.int32, (1, 256), 1)
    not_first = (lane_x > 0).astype(jnp.float32)
    not_last = (lane_x < 255).astype(jnp.float32)

    def shifted(x):
        return [pltpu.roll(x, 1, 1) * not_first, x, pltpu.roll(x, 255, 1) * not_last]

    for z in range(10):
        for ri in range(2):
            if z < 3:
                middle, low, high = (zh_rcv[0, z, ri], ch_rcv[0, 0, z, ri], ch_rcv[0, 1, z, ri])
            elif z < 7:
                middle, low, high = (starts[z - 3][ri], yh_rcv[0, z - 3, ri], yh_rcv[1, z - 3, ri])
            else:
                middle, low, high = (zh_rcv[1, z - 7, ri], ch_rcv[1, 0, z - 7, ri], ch_rcv[1, 1, z - 7, ri])
            grown[z, ri, 0:3, :] = low.astype(jnp.float32)[5:8]
            grown[z, ri, 3:19, :] = middle.astype(jnp.float32)
            grown[z, ri, 19:22, :] = high.astype(jnp.float32)[0:3]

    def valid_rows(rows, each, margin, z, depth):
        y = lax.broadcasted_iota(jnp.int32, (rows, 1), 0) // each + (16 * coil - margin)
        deep = z + (4 * slab - depth)
        good = (y >= 0) & (y < NY) & (deep >= 0) & (deep < NZ)
        return good.astype(jnp.float32)

    def widen(z, _):
        keep = valid_rows(24, 1, 3, z, 3)
        both = [shifted(grown[z, ri] * keep) for ri in range(2)]
        wide_0[z] = jnp.concatenate([both[ri][dx] for dx in range(3) for ri in range(2)], axis=0).astype(jnp.bfloat16)
        return 0

    lax.fori_loop(0, 10, widen, 0)

    def layer_1(z, _):
        hidden = jnp.dot(matrix_1[:, :432], padded_rows(wide_0, z), preferred_element_type=jnp.float32)
        hidden = jnp.maximum(hidden, 0.0) * valid_rows(320, 16, 2, z, 2)
        for dx, moved in enumerate(shifted(hidden)):
            wide_1[z, :, dx] = moved.reshape(20, 16, 256).astype(jnp.bfloat16)
        return 0

    lax.fori_loop(0, 8, layer_1, 0)

    def layer_2(z, _):
        for y in range(18):
            window = wide_1[pl.ds(z, 3), y : y + 3].reshape(432, 256)
            hidden = jnp.dot(weight_2[...], window, preferred_element_type=jnp.float32)
            cell = 16 * coil - 1 + y
            deep = z + 4 * slab - 1
            good = ((cell >= 0) & (cell < NY) & (deep >= 0) & (deep < NZ)).astype(jnp.float32)
            hidden = jnp.maximum(hidden, 0.0) * good
            for dx, moved in enumerate(shifted(hidden)):
                wide_2[z, y, dx] = moved.astype(jnp.bfloat16)
        return 0

    lax.fori_loop(0, 6, layer_2, 0)

    for z in range(4):
        total = None
        for dz in range(3):
            part = jnp.dot(
                matrix_3[dz][:, :864], wide_2[z + dz].reshape(864, 256), preferred_element_type=jnp.float32
            )
            total = part if total is None else total + part
        for ri in range(2):
            refined_out[ri, z] = block[64 * ri + 16 * z : 64 * ri + 16 * z + 16, :] + total[16 * ri : 16 * ri + 16]

    arrived(a_rcv.reshape(256, 8, 128), 3, 255)
    tmp[...] = a_rcv[...].astype(jnp.float32)
    keep = sampled[...].astype(jnp.float32)
    for k in range(4):
        parts = [tmp[:, :, 4 * ri + k, :].reshape(256, 128).T.astype(jnp.bfloat16) for ri in range(2)]
        found = jnp.concatenate(parts, axis=1)
        found = jnp.dot(found, x_h[...], preferred_element_type=jnp.float32) + jnp.dot(
            found, x_l[...], preferred_element_type=jnp.float32
        )
        here = keep[:, k : k + 1]
        residual_out[0, 0, :, k, :] = here * (found[:, :256] - kspace[0, 0, :, k, :])
        residual_out[1, 0, :, k, :] = here * (found[:, 256:] - kspace[1, 0, :, k, :])
    left(i_msg, 0, 31)
    left(s_msg.reshape(256, 8, 128), 1, 255)
    left(y_msg.reshape(256, 8, 128), 2, 255)
    left(a_msg.reshape(256, 8, 128), 3, 255)
    left(c_msg.reshape(256, 1, 128), 4, 255)


OPERANDS = (
    ((2, 4, 128, 256), jnp.float32),
    ((2, 1, 4, 128, 256), jnp.float32),
    ((2, 1, 128, 4, 256), jnp.float32),
    ((128, 4), jnp.int32),
    ((16, 512), jnp.float32),
    ((16, 432), jnp.bfloat16),
    ((8, 896), jnp.float32),
) + (((256, 256), jnp.bfloat16),) * 8 + (((512, 512), jnp.bfloat16),) * 2


def unrolled_step(image, sensitivity, kspace, sampled, w_in, w_mid, w_out):
    base_1 = w_in.astype(jnp.float32).reshape(3, 3, 3, 16, 2).transpose(3, 0, 2, 4, 1)
    base_1 = jnp.pad(base_1, ((0, 0),) * 4 + ((0, 21),)).reshape(16, 432)
    base_1 = jnp.pad(base_1, ((0, 0), (0, 80)))
    weight_2 = w_mid.transpose(1, 0, 2).reshape(16, 432)
    base_3 = w_out.astype(jnp.float32).reshape(3, 9, 2, 16).transpose(0, 2, 1, 3).reshape(6, 144)
    base_3 = jnp.pad(base_3, ((0, 2), (0, 752)))
    operands = (image, sensitivity, kspace, sampled, base_1, weight_2, base_3)
    operands += tuple(jnp.asarray(m) for m in constants())
    whole = pl.BlockSpec(memory_space=pltpu.VMEM)
    message = (32, 8, 8, 128)
    vmem = pltpu.VMEM
    return pl.pallas_call(
        unrolled_kernel,
        out_shape=(
            jax.ShapeDtypeStruct((2, 4, 16, 256), jnp.float32),
            jax.ShapeDtypeStruct((2, 1, 128, 4, 256), jnp.float32),
        ),
        in_specs=[pl.BlockSpec(memory_space=pltpu.HBM)] * len(operands),
        out_specs=(whole, whole),
        scratch_shapes=[vmem(shape, dtype) for shape, dtype in OPERANDS]
        + [pltpu.SemaphoreType.DMA((len(OPERANDS),))]
        + [vmem(message, jnp.int16), vmem(message, jnp.int16)]
        + [vmem((32, 2, 8, 128), jnp.int16), vmem((32, 2, 8, 128), jnp.int16)]
        + [vmem(message, jnp.int16), vmem(message, jnp.int16)]
        + [vmem(message, jnp.bfloat16), vmem(message, jnp.bfloat16)]
        + [vmem((32, 8, 1, 128), jnp.float32), vmem((32, 8, 1, 128), jnp.float32)]
        + [
            vmem(message, jnp.float32),
            vmem((8, 256, 128), jnp.float32),
            vmem((8, 256, 128), jnp.float32),
            vmem((4, 256, 256), jnp.float32),
            vmem((256, 128), jnp.float32),
            vmem((2, 3, 2, 16, 256), jnp.bfloat16),
            vmem((2, 3, 2, 16, 256), jnp.bfloat16),
            vmem((2, 4, 2, 8, 256), jnp.bfloat16),
            vmem((2, 4, 2, 8, 256), jnp.bfloat16),
            vmem((2, 2, 3, 2, 8, 256), jnp.bfloat16),
            vmem((2, 2, 3, 2, 8, 256), jnp.bfloat16),
            vmem((128, 256), jnp.float32),
            vmem((10, 2, 24, 256), jnp.float32),
            vmem((10, 144, 256), jnp.bfloat16),
            vmem((8, 20, 3, 16, 256), jnp.bfloat16),
            vmem((6, 18, 3, 16, 256), jnp.bfloat16),
            vmem((4, 320, 128), jnp.float32),
            vmem((7, 8, 16, 128), jnp.float32),
            vmem((320, 512), jnp.bfloat16),
            vmem((3, 32, 896), jnp.bfloat16),
            pltpu.SemaphoreType.DMA((5,)),
            pltpu.SemaphoreType.DMA((5,)),
            pltpu.SemaphoreType.DMA((8,)),
            pltpu.SemaphoreType.DMA((8,)),
        ],
        compiler_params=pltpu.CompilerParams(
            collective_id=0, has_side_effects=True, vmem_limit_bytes=50 * 1024 * 1024
        ),
        name="unrolled_step",
    )(*operands)


def solution(mesh):
    placed = (
        P(None, "slab", None, None),
        P(None, "coil", "slab", None, None),
        P(None, "coil", None, "slab", None),
        P(None, "slab"),
        P(),
        P(),
        P(),
    )
    return jax.shard_map(
        unrolled_step,
        mesh=mesh,
        in_specs=placed,
        out_specs=(P(None, "slab", "coil", None), P(None, "coil", None, "slab", None)),
        check_vma=False,
    )
```

```python
import functools
import math

import jax
import jax.numpy as jnp
import ml_dtypes
import numpy as np
from jax import lax
from jax.experimental import pallas as pl
from jax.experimental.pallas import tpu as pltpu
from jax.sharding import PartitionSpec as P

NX = 256
NY = 128
NZ = 128

step_size = 0.5
SENS_CODE = 16383.0
IMAGE_CODE = 5461.0
DATA_CODE = 3970.0
MESH = pl.DeviceIdType.MESH


def halves(matrix):
    high = matrix.astype(ml_dtypes.bfloat16)
    low = (matrix - high.astype(np.float64)).astype(ml_dtypes.bfloat16)
    return high, low


def blocks(length, inverse):
    positions = np.arange(length)
    angles = (positions[:, None] * positions[None, :] % length) * (2.0 * math.pi / length)
    cosines = np.cos(angles) / math.sqrt(length)
    sines = np.sin(angles) / math.sqrt(length)
    if inverse:
        sines = -sines
    return np.block([[cosines, sines], [-sines, cosines]])


def mixed_rows(matrix):
    return matrix.reshape(2, 32, 4, -1).transpose(1, 0, 2, 3).reshape(256, -1)


def constants():
    forward = blocks(128, False)
    backward = blocks(128, True)
    made = []
    for matrix in (
        mixed_rows(forward.T).T,
        mixed_rows(forward),
        mixed_rows(backward.T).T,
        mixed_rows(backward),
        blocks(256, True),
    ):
        made.extend(halves(matrix))
    return made


def product(pair, data):
    high = data.astype(jnp.bfloat16)
    low = (data - high.astype(jnp.float32)).astype(jnp.bfloat16)
    first, second = (pair[0][...], pair[1][...])
    dot = functools.partial(jnp.dot, preferred_element_type=jnp.float32)
    return dot(first, high) + (dot(first, low) + dot(second, high))


def product_nt(pair, data):
    high = data.astype(jnp.bfloat16)
    low = (data - high.astype(jnp.float32)).astype(jnp.bfloat16)
    first, second = (pair[0][...], pair[1][...])

    def dot(a, b):
        return lax.dot_general(a, b, (((1,), (1,)), ((), ())), preferred_element_type=jnp.float32)

    return dot(first, high) + (dot(first, low) + dot(second, high))


def regrouped(x):
    parts = []
    for k in range(2):
        lanes = slice(128 * k, 128 * k + 128)
        parts.append(jnp.concatenate([x[:128, lanes], x[128:, lanes]], axis=1))
    return jnp.concatenate(parts, axis=0)


def swapped(x):
    return pltpu.roll(x.reshape(32, 8, 128), 4, 1).reshape(256, 128)


def coded(x, scale):
    return jnp.round(x * scale).astype(jnp.int32).astype(jnp.int16)


def companded(x):
    size = jnp.sqrt(jnp.abs(x)) * DATA_CODE
    return jnp.round(jnp.where(x < 0, -size, size)).astype(jnp.int32).astype(jnp.int16)


def decoded(x):
    return x.astype(jnp.int32).astype(jnp.float32)


def wrapped(value, size):
    return jnp.where(value >= size, value - size, value)


def padded_rows(ref, z):
    return ref[pl.ds(z, 3)].reshape(432, 256)


def unrolled_kernel(*refs):
    count = len(OPERANDS)
    held = refs[count + 2 : 2 * count + 2]
    load_sem = refs[2 * count + 2]
    loads = [pltpu.make_async_copy(refs[k], held[k], load_sem.at[k]) for k in range(count)]
    for load in loads:
        load.start()
    image, sens, kspace, sampled, w_in, w_mid, w_out = held[:7]
    g1f_h, g1f_l, g2f_h, g2f_l, g1i_h, g1i_l, g2i_h, g2i_l, x_h, x_l = held[7:]
    refined_out, residual_out = refs[count : count + 2]
    (
        s_msg, s_rcv, i_msg, i_rcv, y_msg, y_rcv, a_msg, a_rcv, c_msg, c_rcv,
        tmp, sens_a, sens_b, spec, cur,
        zh_msg, zh_rcv, yh_msg, yh_rcv, ch_msg, ch_rcv,
        block, grown, wide_0, wide_1, wide_2, toeplitz_1, toeplitz_3, matrix_1, matrix_3, base_1, base_3, weight_2,
        send_sem, recv_sem, halo_send, halo_recv,
    ) = refs[2 * count + 3 :]
    slab = lax.axis_index("slab")
    coil = lax.axis_index("coil")
    g1f, g2f, g1i, g2i, gx = ((g1f_h, g1f_l), (g2f_h, g2f_l), (g1i_h, g1i_l), (g2i_h, g2i_l), (x_h, x_l))

    coils = [wrapped(coil + k, 8) for k in (4, 5, 3, 2, 6, 7, 1, 0)]

    def every_other(act, first=0, last=16):
        def rings(k, _):
            step = (k + 1) // 2 * (2 * lax.rem(k, 2) - 1)
            for s in (wrapped(slab + 8 + step, 32), wrapped(slab + 24 + step, 32)):
                for c in coils:
                    act(s, c)
            return 0

        lax.fori_loop(first, min(last, 15), rings, 0)
        if last == 16:
            for c in coils:
                act(wrapped(slab + 16, 32), c)
            for c in coils[:7]:
                act(slab, c)

    barrier = pltpu.get_barrier_semaphore()
    every_other(
        lambda s, c: pl.semaphore_signal(barrier, inc=1, device_id={"slab": s, "coil": c}, device_id_type=MESH)
    )

    def arrived(flat, which, count):
        part = flat.at[pl.ds(0, count)]
        pltpu.make_async_copy(part, part, recv_sem.at[which]).wait()

    def left(flat, which, count):
        part = flat.at[pl.ds(0, count)]
        pltpu.make_async_copy(part, part, send_sem.at[which]).wait()

    def send_all(msg, rcv, which, first=0, last=16):
        every_other(
            lambda s, c: pltpu.make_async_remote_copy(
                msg.at[s, c], rcv.at[slab, coil], send_sem.at[which], recv_sem.at[which],
                device_id={"slab": s, "coil": c}, device_id_type=MESH,
            ).start(),
            first,
            last,
        )
        if last == 16:
            rcv[slab, coil] = msg[slab, coil]

    loads[1].wait()
    for ri in range(2):
        for z in range(4):
            tmp[:, :, ri * 4 + z, :] = sens[ri, 0, z].T.reshape(32, 8, 128)
    s_msg[...] = coded(tmp[...], SENS_CODE)
    loads[0].wait()
    loads[3].wait()
    for ri in range(2):
        for z in range(4):
            tmp[:, :, ri * 4 + z, :] = image[ri, z].T.reshape(32, 8, 128)
    mask = sampled[...].astype(jnp.float32)
    mask = jnp.concatenate([mask, mask], axis=0)
    own = coded(tmp[:, coil], IMAGE_CODE)
    i_msg[:, 0] = own
    i_msg[:, 1] = jnp.broadcast_to(coded(mask, 1.0)[None], (32, 8, 128))

    for number in (2, *range(4, count)):
        loads[number].wait()
    tap = lax.broadcasted_iota(jnp.int32, (27, 512), 0)
    lane = lax.broadcasted_iota(jnp.int32, (27, 512), 1)
    tap_z, tap_y, tap_x = (tap // 9, lax.rem(tap // 3, 3), lax.rem(tap, 3))

    def placed(taps, spot):
        return jnp.dot(taps, (lane == spot).astype(jnp.float32), preferred_element_type=jnp.float32)

    taps_1, taps_2, taps_3 = (w[...].astype(jnp.float32) for w in (w_in, w_mid, w_out))
    base_1[...] = sum(placed(taps_1[:, ri, :], 144 * tap_z + 24 * (2 * tap_x + ri) + tap_y) for ri in range(2))
    weight_2[...] = sum(placed(taps_2[:, i, :], 16 * tap + i) for i in range(16)).astype(jnp.bfloat16)
    spread_3 = sum(placed(taps_3[:, i, :], 16 * tap + i) for i in range(16))
    base_3[...] = jnp.zeros((8, 896), jnp.float32)
    for dz in range(3):
        base_3[2 * dz : 2 * dz + 2, 0:144] = spread_3[:, 144 * dz : 144 * dz + 144]
    for o in range(16):
        spread = jnp.broadcast_to(base_1[o : o + 1, :], (24, 512))
        turned = pltpu.roll(spread, 0, 1, stride=1, stride_axis=0)
        for part in range(4):
            toeplitz_1[part, pl.ds(o, 20, stride=16), :] = turned[:20, 128 * part : 128 * part + 128]
    for part in range(4):
        matrix_1[:, 128 * part : 128 * part + 128] = toeplitz_1[part].astype(jnp.bfloat16)
    for y in range(16):
        turned = pltpu.roll(base_3[...], 48 * y, 1) if y else base_3[...]
        for part in range(7):
            toeplitz_3[part, :, y, :] = turned[:, 128 * part : 128 * part + 128]
    for dz in range(3):
        for ri in range(2):
            for part in range(7):
                matrix_3[dz, 16 * ri : 16 * ri + 16, 128 * part : 128 * part + 128] = toeplitz_3[
                    part, 2 * dz + ri
                ].astype(jnp.bfloat16)
    grown[...] = jnp.zeros((10, 2, 24, 256), jnp.float32)

    pl.semaphore_wait(barrier, 255)

    def send_image(k, _):
        s = wrapped(slab + k, 32)
        pltpu.make_async_remote_copy(
            i_msg.at[s], i_rcv.at[slab], send_sem.at[0], recv_sem.at[0],
            device_id={"slab": s, "coil": coil}, device_id_type=MESH,
        ).start()
        return 0

    lax.fori_loop(1, 32, send_image, 0)
    i_rcv[slab] = i_msg[slab]
    send_all(s_msg, s_rcv, 1)

    stacked = jnp.concatenate(
        [jnp.concatenate([kspace[0, 0, :, k, :], kspace[1, 0, :, k, :]], axis=1) for k in range(4)], axis=0
    )
    hybrid = product_nt(gx, stacked)
    for ri in range(2):
        for k in range(4):
            tmp[:, :, ri * 4 + k, :] = hybrid[256 * ri : 256 * ri + 256, 128 * k : 128 * k + 128].reshape(32, 8, 128)
    y_msg[...] = companded(tmp[...])
    send_all(y_msg, y_rcv, 2)

    arrived(i_rcv, 0, 31)
    arrived(s_rcv.reshape(256, 8, 128), 1, 255)
    cur[...] = decoded(i_rcv[:, 0]).reshape(256, 128) * (1.0 / IMAGE_CODE)

    lower = lax.broadcasted_iota(jnp.int32, (256, 128), 0) % 8 < 4

    def unpack(c, _):
        both = decoded(s_rcv[:, c]).reshape(256, 128) * (1.0 / SENS_CODE)
        other = swapped(both)
        sens_a[c] = jnp.where(lower, both, other)
        sens_b[c] = jnp.where(lower, -other, both)
        return 0

    lax.fori_loop(0, 8, unpack, 0)

    def forward(p, now, turned):
        c = 2 * p
        v = jnp.concatenate(
            [sens_a[c] * now + sens_b[c] * turned, sens_a[c + 1] * now + sens_b[c + 1] * turned], axis=1
        )
        return product_nt(g2f, regrouped(product(g1f, v)))

    def backward(p, found, weight):
        c = 2 * p
        res = []
        for k in range(2):
            code = decoded(y_rcv[:, c + k]).reshape(256, 128)
            data = code * jnp.abs(code) * (1.0 / DATA_CODE**2)
            res.append(weight * (found[:, 128 * k : 128 * k + 128] - data))
        b = product_nt(g2i, regrouped(product(g1i, jnp.concatenate(res, axis=1))))
        total = None
        for k in range(2):
            part = b[:, 128 * k : 128 * k + 128]
            term = sens_a[c + k] * part - sens_b[c + k] * swapped(part)
            total = term if total is None else total + term
        return total

    now = cur[...]
    turned = swapped(now)

    def ahead(p, _):
        spec[p] = forward(p, now, turned)
        return 0

    lax.fori_loop(0, 4, ahead, 0)
    arrived(y_rcv.reshape(256, 8, 128), 2, 255)
    weight = decoded(i_rcv[:, 1]).reshape(256, 128)
    grad = lax.fori_loop(0, 4, lambda p, g: g + backward(p, spec[p], weight), jnp.zeros((256, 128), jnp.float32))
    now_1 = now - step_size * grad
    turned_1 = swapped(now_1)

    def again(p, g):
        found = forward(p, now_1, turned_1)
        for k in range(2):
            a_msg[:, 2 * p + k] = found[:, 128 * k : 128 * k + 128].reshape(32, 8, 128).astype(jnp.bfloat16)
        return g + backward(p, found, weight)

    grad = lax.fori_loop(0, 4, again, jnp.zeros((256, 128), jnp.float32))
    cur[...] = now_1 - step_size * grad

    lane_block = lax.broadcasted_iota(jnp.int32, (32, 128), 1) // 16
    picked = [cur[pl.ds(r, 32, stride=8), :] for r in range(8)]
    for c in range(8):
        packed = None
        for r in range(8):
            shift = 16 * ((r - c) % 8)
            moved = pltpu.roll(picked[r], shift, 1) if shift else picked[r]
            packed = moved if packed is None else jnp.where(lane_block == r, moved, packed)
        c_msg[:, c, 0, :] = packed
    send_all(c_msg, c_rcv, 4)
    send_all(a_msg, a_rcv, 3, 0, 6)
    arrived(c_rcv.reshape(256, 1, 128), 4, 255)
    block[...] = c_rcv[:, :, 0, :].reshape(256, 128).T

    starts = [[block[64 * ri + 16 * z : 64 * ri + 16 * z + 16, :] for ri in range(2)] for z in range(4)]
    for z in range(4):
        for ri in range(2):
            first = starts[z][ri][:8].astype(jnp.bfloat16)
            last = starts[z][ri][8:].astype(jnp.bfloat16)
            yh_msg[0, z, ri] = first
            yh_msg[1, z, ri] = last
            for side in range(2):
                if 0 <= z - side < 3:
                    zh_msg[side, z - side, ri] = starts[z][ri].astype(jnp.bfloat16)
                    ch_msg[side, 0, z - side, ri] = first
                    ch_msg[side, 1, z - side, ri] = last

    halos = []
    for side in range(2):
        s = lax.rem(slab + (31 if side == 0 else 1), 32)
        c = lax.rem(coil + (7 if side == 0 else 1), 8)
        halos.append((zh_msg.at[side], zh_rcv.at[1 - side], s, coil))
        halos.append((yh_msg.at[side], yh_rcv.at[1 - side], slab, c))
        for other in range(2):
            c = lax.rem(coil + (7 if other == 0 else 1), 8)
            halos.append((ch_msg.at[side, other], ch_rcv.at[1 - side, 1 - other], s, c))
    halos = [
        pltpu.make_async_remote_copy(
            src, dst, halo_send.at[k], halo_recv.at[k], device_id={"slab": s, "coil": c}, device_id_type=MESH
        )
        for k, (src, dst, s, c) in enumerate(halos)
    ]
    for halo in halos:
        halo.start()
    send_all(a_msg, a_rcv, 3, 6, 16)
    for halo in halos:
        halo.wait()

    lane_x = lax.broadcasted_iota(jnp.int32, (1, 256), 1)
    not_first = (lane_x > 0).astype(jnp.float32)
    not_last = (lane_x < 255).astype(jnp.float32)

    def shifted(x):
        return [pltpu.roll(x, 1, 1) * not_first, x, pltpu.roll(x, 255, 1) * not_last]

    for z in range(10):
        for ri in range(2):
            if z < 3:
                middle, low, high = (zh_rcv[0, z, ri], ch_rcv[0, 0, z, ri], ch_rcv[0, 1, z, ri])
            elif z < 7:
                middle, low, high = (starts[z - 3][ri], yh_rcv[0, z - 3, ri], yh_rcv[1, z - 3, ri])
            else:
                middle, low, high = (zh_rcv[1, z - 7, ri], ch_rcv[1, 0, z - 7, ri], ch_rcv[1, 1, z - 7, ri])
            grown[z, ri, 0:3, :] = low.astype(jnp.float32)[5:8]
            grown[z, ri, 3:19, :] = middle.astype(jnp.float32)
            grown[z, ri, 19:22, :] = high.astype(jnp.float32)[0:3]

    def valid_rows(rows, each, margin, z, depth):
        y = lax.broadcasted_iota(jnp.int32, (rows, 1), 0) // each + (16 * coil - margin)
        deep = z + (4 * slab - depth)
        good = (y >= 0) & (y < NY) & (deep >= 0) & (deep < NZ)
        return good.astype(jnp.float32)

    def widen(z, _):
        keep = valid_rows(24, 1, 3, z, 3)
        both = [shifted(grown[z, ri] * keep) for ri in range(2)]
        wide_0[z] = jnp.concatenate([both[ri][dx] for dx in range(3) for ri in range(2)], axis=0).astype(jnp.bfloat16)
        return 0

    lax.fori_loop(0, 10, widen, 0)

    def layer_1(z, _):
        hidden = jnp.dot(matrix_1[:, :432], padded_rows(wide_0, z), preferred_element_type=jnp.float32)
        hidden = jnp.maximum(hidden, 0.0) * valid_rows(320, 16, 2, z, 2)
        for dx, moved in enumerate(shifted(hidden)):
            wide_1[z, :, dx] = moved.reshape(20, 16, 256).astype(jnp.bfloat16)
        return 0

    lax.fori_loop(0, 8, layer_1, 0)

    def layer_2(z, _):
        for y in range(18):
            window = wide_1[pl.ds(z, 3), y : y + 3].reshape(432, 256)
            hidden = jnp.dot(weight_2[:, :432], window, preferred_element_type=jnp.float32)
            cell = 16 * coil - 1 + y
            deep = z + 4 * slab - 1
            good = ((cell >= 0) & (cell < NY) & (deep >= 0) & (deep < NZ)).astype(jnp.float32)
            hidden = jnp.maximum(hidden, 0.0) * good
            for dx, moved in enumerate(shifted(hidden)):
                wide_2[z, y, dx] = moved.astype(jnp.bfloat16)
        return 0

    lax.fori_loop(0, 6, layer_2, 0)

    for z in range(4):
        total = None
        for dz in range(3):
            part = jnp.dot(
                matrix_3[dz][:, :864], wide_2[z + dz].reshape(864, 256), preferred_element_type=jnp.float32
            )
            total = part if total is None else total + part
        for ri in range(2):
            refined_out[ri, z] = block[64 * ri + 16 * z : 64 * ri + 16 * z + 16, :] + total[16 * ri : 16 * ri + 16]

    arrived(a_rcv.reshape(256, 8, 128), 3, 255)
    tmp[...] = a_rcv[...].astype(jnp.float32)
    rows = lax.broadcasted_iota(jnp.int32, (128, 128), 0)
    columns = lax.broadcasted_iota(jnp.int32, (128, 128), 1)
    keep = lax.dot_general(
        (rows == columns).astype(jnp.float32), mask, (((1,), (1,)), ((), ())), preferred_element_type=jnp.float32
    )
    for k in range(4):
        parts = [tmp[:, :, 4 * ri + k, :].reshape(256, 128).T.astype(jnp.bfloat16) for ri in range(2)]
        found = jnp.concatenate(parts, axis=1)
        found = jnp.dot(found, x_h[...], preferred_element_type=jnp.float32) + jnp.dot(
            found, x_l[...], preferred_element_type=jnp.float32
        )
        here = keep[:, k : k + 1]
        residual_out[0, 0, :, k, :] = here * (found[:, :256] - kspace[0, 0, :, k, :])
        residual_out[1, 0, :, k, :] = here * (found[:, 256:] - kspace[1, 0, :, k, :])
    left(i_msg, 0, 31)
    left(s_msg.reshape(256, 8, 128), 1, 255)
    left(y_msg.reshape(256, 8, 128), 2, 255)
    left(a_msg.reshape(256, 8, 128), 3, 255)
    left(c_msg.reshape(256, 1, 128), 4, 255)


OPERANDS = (
    ((2, 4, 128, 256), jnp.float32),
    ((2, 1, 4, 128, 256), jnp.float32),
    ((2, 1, 128, 4, 256), jnp.float32),
    ((4, 128), jnp.int32),
    ((16, 2, 27), jnp.bfloat16),
    ((16, 16, 27), jnp.bfloat16),
    ((2, 16, 27), jnp.bfloat16),
) + (((256, 256), jnp.bfloat16),) * 8 + (((512, 512), jnp.bfloat16),) * 2


def unrolled_step(image, sensitivity, kspace, sampled, w_in, w_mid, w_out):
    operands = (image, sensitivity, kspace, sampled.T) + tuple(
        w.transpose(1, 2, 0) for w in (w_in, w_mid, w_out)
    )
    operands += tuple(jnp.asarray(m) for m in constants())
    whole = pl.BlockSpec(memory_space=pltpu.VMEM)
    message = (32, 8, 8, 128)
    vmem = pltpu.VMEM
    return pl.pallas_call(
        unrolled_kernel,
        out_shape=(
            jax.ShapeDtypeStruct((2, 4, 16, 256), jnp.float32),
            jax.ShapeDtypeStruct((2, 1, 128, 4, 256), jnp.float32),
        ),
        in_specs=[pl.BlockSpec(memory_space=pltpu.HBM)] * len(operands),
        out_specs=(whole, whole),
        scratch_shapes=[vmem(shape, dtype) for shape, dtype in OPERANDS]
        + [pltpu.SemaphoreType.DMA((len(OPERANDS),))]
        + [vmem(message, jnp.int16), vmem(message, jnp.int16)]
        + [vmem((32, 2, 8, 128), jnp.int16), vmem((32, 2, 8, 128), jnp.int16)]
        + [vmem(message, jnp.int16), vmem(message, jnp.int16)]
        + [vmem(message, jnp.bfloat16), vmem(message, jnp.bfloat16)]
        + [vmem((32, 8, 1, 128), jnp.float32), vmem((32, 8, 1, 128), jnp.float32)]
        + [
            vmem(message, jnp.float32),
            vmem((8, 256, 128), jnp.float32),
            vmem((8, 256, 128), jnp.float32),
            vmem((4, 256, 256), jnp.float32),
            vmem((256, 128), jnp.float32),
            vmem((2, 3, 2, 16, 256), jnp.bfloat16),
            vmem((2, 3, 2, 16, 256), jnp.bfloat16),
            vmem((2, 4, 2, 8, 256), jnp.bfloat16),
            vmem((2, 4, 2, 8, 256), jnp.bfloat16),
            vmem((2, 2, 3, 2, 8, 256), jnp.bfloat16),
            vmem((2, 2, 3, 2, 8, 256), jnp.bfloat16),
            vmem((128, 256), jnp.float32),
            vmem((10, 2, 24, 256), jnp.float32),
            vmem((10, 144, 256), jnp.bfloat16),
            vmem((8, 20, 3, 16, 256), jnp.bfloat16),
            vmem((6, 18, 3, 16, 256), jnp.bfloat16),
            vmem((4, 320, 128), jnp.float32),
            vmem((7, 8, 16, 128), jnp.float32),
            vmem((320, 512), jnp.bfloat16),
            vmem((3, 32, 896), jnp.bfloat16),
            vmem((16, 512), jnp.float32),
            vmem((8, 896), jnp.float32),
            vmem((16, 512), jnp.bfloat16),
            pltpu.SemaphoreType.DMA((5,)),
            pltpu.SemaphoreType.DMA((5,)),
            pltpu.SemaphoreType.DMA((8,)),
            pltpu.SemaphoreType.DMA((8,)),
        ],
        compiler_params=pltpu.CompilerParams(
            collective_id=0, has_side_effects=True, vmem_limit_bytes=52 * 1024 * 1024
        ),
        name="unrolled_step",
    )(*(pltpu.with_memory_space_constraint(x, pltpu.HBM) for x in operands))


def solution(mesh):
    placed = (
        P(None, "slab", None, None),
        P(None, "coil", "slab", None, None),
        P(None, "coil", None, "slab", None),
        P(None, "slab"),
        P(),
        P(),
        P(),
    )
    return jax.shard_map(
        unrolled_step,
        mesh=mesh,
        in_specs=placed,
        out_specs=(P(None, "slab", "coil", None), P(None, "coil", None, "slab", None)),
        check_vma=False,
    )
```

```python
import functools
import math

import jax
import jax.numpy as jnp
import ml_dtypes
import numpy as np
from jax import lax
from jax.experimental import pallas as pl
from jax.experimental.pallas import tpu as pltpu
from jax.sharding import PartitionSpec as P

NX = 256
NY = 128
NZ = 128

step_size = 0.5
SENS_CODE = 16383.0
IMAGE_CODE = 5461.0
DATA_CODE = 3970.0
MESH = pl.DeviceIdType.MESH


def halves(matrix):
    high = matrix.astype(ml_dtypes.bfloat16)
    low = (matrix - high.astype(np.float64)).astype(ml_dtypes.bfloat16)
    return high, low


def blocks(length, inverse):
    positions = np.arange(length)
    angles = (positions[:, None] * positions[None, :] % length) * (2.0 * math.pi / length)
    cosines = np.cos(angles) / math.sqrt(length)
    sines = np.sin(angles) / math.sqrt(length)
    if inverse:
        sines = -sines
    return np.block([[cosines, sines], [-sines, cosines]])


def mixed_rows(matrix):
    return matrix.reshape(2, 32, 4, -1).transpose(1, 0, 2, 3).reshape(256, -1)


def constants():
    forward = blocks(128, False)
    backward = blocks(128, True)
    made = []
    for matrix in (
        mixed_rows(forward.T).T,
        mixed_rows(forward),
        mixed_rows(backward.T).T,
        mixed_rows(backward),
        blocks(256, True),
    ):
        made.extend(halves(matrix))
    return made


def product(pair, data):
    high = data.astype(jnp.bfloat16)
    low = (data - high.astype(jnp.float32)).astype(jnp.bfloat16)
    first, second = (pair[0][...], pair[1][...])
    dot = functools.partial(jnp.dot, preferred_element_type=jnp.float32)
    return dot(first, high) + (dot(first, low) + dot(second, high))


def product_nt(pair, data):
    high = data.astype(jnp.bfloat16)
    low = (data - high.astype(jnp.float32)).astype(jnp.bfloat16)
    first, second = (pair[0][...], pair[1][...])

    def dot(a, b):
        return lax.dot_general(a, b, (((1,), (1,)), ((), ())), preferred_element_type=jnp.float32)

    return dot(first, high) + (dot(first, low) + dot(second, high))


def regrouped(x):
    parts = []
    for k in range(2):
        lanes = slice(128 * k, 128 * k + 128)
        parts.append(jnp.concatenate([x[:128, lanes], x[128:, lanes]], axis=1))
    return jnp.concatenate(parts, axis=0)


def swapped(x):
    return pltpu.roll(x.reshape(32, 8, 128), 4, 1).reshape(256, 128)


def coded(x, scale):
    return jnp.round(x * scale).astype(jnp.int32).astype(jnp.int16)


def companded(x):
    size = jnp.sqrt(jnp.abs(x)) * DATA_CODE
    return jnp.round(jnp.where(x < 0, -size, size)).astype(jnp.int32).astype(jnp.int16)


def decoded(x):
    return x.astype(jnp.int32).astype(jnp.float32)


def wrapped(value, size):
    return jnp.where(value >= size, value - size, value)


def padded_rows(ref, z):
    return ref[pl.ds(z, 3)].reshape(432, 256)


def unrolled_kernel(*refs):
    count = len(OPERANDS)
    held = refs[count + 2 : 2 * count + 2]
    load_sem = refs[2 * count + 2]
    loads = [pltpu.make_async_copy(refs[k], held[k], load_sem.at[k]) for k in range(count)]
    for load in loads:
        load.start()
    image, sens, kspace, sampled, w_in, w_mid, w_out = held[:7]
    g1f_h, g1f_l, g2f_h, g2f_l, g1i_h, g1i_l, g2i_h, g2i_l, x_h, x_l = held[7:]
    refined_out, residual_out = refs[count : count + 2]
    (
        s_msg, s_rcv, i_msg, i_rcv, y_msg, y_rcv, a_msg, a_rcv, c_msg, c_rcv,
        tmp, sens_a, sens_b, spec, cur,
        zh_msg, zh_rcv, yh_msg, yh_rcv, ch_msg, ch_rcv,
        block, grown, wide_0, wide_1, wide_2, toeplitz_1, toeplitz_3, matrix_1, matrix_2, matrix_3, base_3,
        send_sem, recv_sem, halo_send, halo_recv,
    ) = refs[2 * count + 3 :]
    slab = lax.axis_index("slab")
    coil = lax.axis_index("coil")
    g1f, g2f, g1i, g2i, gx = ((g1f_h, g1f_l), (g2f_h, g2f_l), (g1i_h, g1i_l), (g2i_h, g2i_l), (x_h, x_l))

    coils = [wrapped(coil + k, 8) for k in (4, 5, 3, 2, 6, 7, 1, 0)]

    def every_other(act, first=0, last=16):
        def rings(k, _):
            step = (k + 1) // 2 * (2 * lax.rem(k, 2) - 1)
            for s in (wrapped(slab + 8 + step, 32), wrapped(slab + 24 + step, 32)):
                for c in coils:
                    act(s, c)
            return 0

        lax.fori_loop(first, min(last, 15), rings, 0)
        if last == 16:
            for c in coils:
                act(wrapped(slab + 16, 32), c)
            for c in coils[:7]:
                act(slab, c)

    barrier = pltpu.get_barrier_semaphore()
    every_other(
        lambda s, c: pl.semaphore_signal(barrier, inc=1, device_id={"slab": s, "coil": c}, device_id_type=MESH)
    )

    def arrived(flat, which, count):
        part = flat.at[pl.ds(0, count)]
        pltpu.make_async_copy(part, part, recv_sem.at[which]).wait()

    def left(flat, which, count):
        part = flat.at[pl.ds(0, count)]
        pltpu.make_async_copy(part, part, send_sem.at[which]).wait()

    def send_all(msg, rcv, which, first=0, last=16):
        every_other(
            lambda s, c: pltpu.make_async_remote_copy(
                msg.at[s, c], rcv.at[slab, coil], send_sem.at[which], recv_sem.at[which],
                device_id={"slab": s, "coil": c}, device_id_type=MESH,
            ).start(),
            first,
            last,
        )
        if last == 16:
            rcv[slab, coil] = msg[slab, coil]

    loads[1].wait()
    for ri in range(2):
        for z in range(4):
            tmp[:, :, ri * 4 + z, :] = sens[ri, 0, z].T.reshape(32, 8, 128)
    s_msg[...] = coded(tmp[...], SENS_CODE)
    loads[0].wait()
    loads[3].wait()
    for ri in range(2):
        for z in range(4):
            tmp[:, :, ri * 4 + z, :] = image[ri, z].T.reshape(32, 8, 128)
    mask = sampled[...].astype(jnp.float32)
    mask = jnp.concatenate([mask, mask], axis=0)
    own = coded(tmp[:, coil], IMAGE_CODE)
    i_msg[:, 0] = own
    i_msg[:, 1] = jnp.broadcast_to(coded(mask, 1.0)[None], (32, 8, 128))

    for number in (2, *range(4, count)):
        loads[number].wait()
    tap = lax.broadcasted_iota(jnp.int32, (27, 1024), 0)
    lane = lax.broadcasted_iota(jnp.int32, (27, 1024), 1)
    tap_z, tap_y, tap_x = (tap // 9, lax.rem(tap // 3, 3), lax.rem(tap, 3))

    def placed(taps, spot):
        here = (lane == spot).astype(jnp.float32)[:, : 128 * spot_parts]
        return jnp.dot(taps, here, preferred_element_type=jnp.float32)

    def in_grid(y):
        return ((y >= 0) & (y < NY)).astype(jnp.float32)

    taps_1, taps_2, taps_3 = (w[...].astype(jnp.float32) for w in (w_in, w_mid, w_out))
    spot_parts = 4
    base_1 = sum(placed(taps_1[:, ri, :], 144 * tap_z + 24 * (2 * tap_x + ri) + tap_y) for ri in range(2))
    good = in_grid(lax.broadcasted_iota(jnp.int32, (24, 1), 0) + (16 * coil - 2))
    for o in range(16):
        spread = jnp.broadcast_to(base_1[o : o + 1, :], (24, 512))
        turned = pltpu.roll(spread, 0, 1, stride=1, stride_axis=0) * good
        for part in range(4):
            toeplitz_1[part, pl.ds(o, 20, stride=16), :] = turned[:20, 128 * part : 128 * part + 128]
    for part in range(4):
        matrix_1[:, 128 * part : 128 * part + 128] = toeplitz_1[part].astype(jnp.bfloat16)
    spot_parts = 8
    for dx in range(3):
        base_2 = sum(
            placed(taps_2[:, i, :], jnp.where(tap_x == dx, 320 * tap_z + 16 * tap_y + i, -1)) for i in range(16)
        )
        for y in range(18):
            turned = pltpu.roll(base_2, 16 * y, 1) if y else base_2
            first = 288 * dx + 16 * y
            matrix_2[first : first + 16, :] = (turned * in_grid(16 * coil - 1 + y)).astype(jnp.bfloat16)
    spot_parts = 7
    for dx in range(3):
        base_3[2 * dx : 2 * dx + 2, :] = sum(
            placed(taps_3[:, i, :], jnp.where(tap_x == dx, 288 * tap_z + 16 * tap_y + i, -1)) for i in range(16)
        )
    base_3[6:8, :] = jnp.zeros((2, 896), jnp.float32)
    for y in range(16):
        turned = pltpu.roll(base_3[...], 16 * y, 1) if y else base_3[...]
        for part in range(7):
            toeplitz_3[part, :, y, :] = turned[:, 128 * part : 128 * part + 128]
    for part in range(7):
        matrix_3[:, 128 * part : 128 * part + 128] = toeplitz_3[part, 0:6].reshape(96, 128).astype(jnp.bfloat16)
    grown[...] = jnp.zeros((10, 2, 24, 256), jnp.float32)

    pl.semaphore_wait(barrier, 255)

    def send_image(k, _):
        s = wrapped(slab + k, 32)
        pltpu.make_async_remote_copy(
            i_msg.at[s], i_rcv.at[slab], send_sem.at[0], recv_sem.at[0],
            device_id={"slab": s, "coil": coil}, device_id_type=MESH,
        ).start()
        return 0

    lax.fori_loop(1, 32, send_image, 0)
    i_rcv[slab] = i_msg[slab]
    send_all(s_msg, s_rcv, 1)

    stacked = jnp.concatenate(
        [jnp.concatenate([kspace[0, 0, :, k, :], kspace[1, 0, :, k, :]], axis=1) for k in range(4)], axis=0
    )
    hybrid = product_nt(gx, stacked)
    for ri in range(2):
        for k in range(4):
            tmp[:, :, ri * 4 + k, :] = hybrid[256 * ri : 256 * ri + 256, 128 * k : 128 * k + 128].reshape(32, 8, 128)
    y_msg[...] = companded(tmp[...])
    send_all(y_msg, y_rcv, 2)

    arrived(i_rcv, 0, 31)
    arrived(s_rcv.reshape(256, 8, 128), 1, 255)
    cur[...] = decoded(i_rcv[:, 0]).reshape(256, 128) * (1.0 / IMAGE_CODE)

    lower = lax.broadcasted_iota(jnp.int32, (256, 128), 0) % 8 < 4

    def unpack(c, _):
        both = decoded(s_rcv[:, c]).reshape(256, 128) * (1.0 / SENS_CODE)
        other = swapped(both)
        sens_a[c] = jnp.where(lower, both, other)
        sens_b[c] = jnp.where(lower, -other, both)
        return 0

    lax.fori_loop(0, 8, unpack, 0)

    def forward(p, now, turned):
        c = 2 * p
        v = jnp.concatenate(
            [sens_a[c] * now + sens_b[c] * turned, sens_a[c + 1] * now + sens_b[c + 1] * turned], axis=1
        )
        return product_nt(g2f, regrouped(product(g1f, v)))

    def backward(p, found, weight):
        c = 2 * p
        res = []
        for k in range(2):
            code = decoded(y_rcv[:, c + k]).reshape(256, 128)
            data = code * jnp.abs(code) * (1.0 / DATA_CODE**2)
            res.append(weight * (found[:, 128 * k : 128 * k + 128] - data))
        b = product_nt(g2i, regrouped(product(g1i, jnp.concatenate(res, axis=1))))
        total = None
        for k in range(2):
            part = b[:, 128 * k : 128 * k + 128]
            term = sens_a[c + k] * part - sens_b[c + k] * swapped(part)
            total = term if total is None else total + term
        return total

    now = cur[...]
    turned = swapped(now)

    def ahead(p, _):
        spec[p] = forward(p, now, turned)
        return 0

    lax.fori_loop(0, 4, ahead, 0, unroll=2)
    arrived(y_rcv.reshape(256, 8, 128), 2, 255)
    weight = decoded(i_rcv[:, 1]).reshape(256, 128)

    def add_back(p, g):
        return g + backward(p, spec[p], weight)

    grad = lax.fori_loop(0, 4, add_back, jnp.zeros((256, 128), jnp.float32), unroll=4)
    now_1 = now - step_size * grad
    turned_1 = swapped(now_1)

    def again(p, _):
        found = forward(p, now_1, turned_1)
        for k in range(2):
            a_msg[:, 2 * p + k] = found[:, 128 * k : 128 * k + 128].reshape(32, 8, 128).astype(jnp.bfloat16)
        spec[p] = found
        return 0

    lax.fori_loop(0, 4, again, 0, unroll=4)
    send_all(a_msg, a_rcv, 3, 0, 3)
    grad = lax.fori_loop(0, 4, add_back, jnp.zeros((256, 128), jnp.float32), unroll=4)
    cur[...] = now_1 - step_size * grad

    lane_block = lax.broadcasted_iota(jnp.int32, (32, 128), 1) // 16
    picked = [cur[pl.ds(r, 32, stride=8), :] for r in range(8)]
    for c in range(8):
        packed = None
        for r in range(8):
            shift = 16 * ((r - c) % 8)
            moved = pltpu.roll(picked[r], shift, 1) if shift else picked[r]
            packed = moved if packed is None else jnp.where(lane_block == r, moved, packed)
        c_msg[:, c, 0, :] = packed
    send_all(c_msg, c_rcv, 4)
    send_all(a_msg, a_rcv, 3, 3, 10)
    arrived(c_rcv.reshape(256, 1, 128), 4, 255)
    block[...] = c_rcv[:, :, 0, :].reshape(256, 128).T

    starts = [[block[64 * ri + 16 * z : 64 * ri + 16 * z + 16, :] for ri in range(2)] for z in range(4)]
    for z in range(4):
        for ri in range(2):
            first = starts[z][ri][:8].astype(jnp.bfloat16)
            last = starts[z][ri][8:].astype(jnp.bfloat16)
            yh_msg[0, z, ri] = first
            yh_msg[1, z, ri] = last
            for side in range(2):
                if 0 <= z - side < 3:
                    zh_msg[side, z - side, ri] = starts[z][ri].astype(jnp.bfloat16)
                    ch_msg[side, 0, z - side, ri] = first
                    ch_msg[side, 1, z - side, ri] = last

    halos = []
    for side in range(2):
        s = lax.rem(slab + (31 if side == 0 else 1), 32)
        c = lax.rem(coil + (7 if side == 0 else 1), 8)
        halos.append((zh_msg.at[side], zh_rcv.at[1 - side], s, coil))
        halos.append((yh_msg.at[side], yh_rcv.at[1 - side], slab, c))
        for other in range(2):
            c = lax.rem(coil + (7 if other == 0 else 1), 8)
            halos.append((ch_msg.at[side, other], ch_rcv.at[1 - side, 1 - other], s, c))
    halos = [
        pltpu.make_async_remote_copy(
            src, dst, halo_send.at[k], halo_recv.at[k], device_id={"slab": s, "coil": c}, device_id_type=MESH
        )
        for k, (src, dst, s, c) in enumerate(halos)
    ]
    for halo in halos:
        halo.start()
    send_all(a_msg, a_rcv, 3, 10, 16)
    for halo in halos:
        halo.wait()

    lane_x = lax.broadcasted_iota(jnp.int32, (1, 256), 1)
    not_first = (lane_x > 0).astype(jnp.float32)
    not_last = (lane_x < 255).astype(jnp.float32)

    def shifted(x):
        return [pltpu.roll(x, 1, 1) * not_first, x, pltpu.roll(x, 255, 1) * not_last]

    for z in range(10):
        for ri in range(2):
            if z < 3:
                middle, low, high = (zh_rcv[0, z, ri], ch_rcv[0, 0, z, ri], ch_rcv[0, 1, z, ri])
            elif z < 7:
                middle, low, high = (starts[z - 3][ri], yh_rcv[0, z - 3, ri], yh_rcv[1, z - 3, ri])
            else:
                middle, low, high = (zh_rcv[1, z - 7, ri], ch_rcv[1, 0, z - 7, ri], ch_rcv[1, 1, z - 7, ri])
            grown[z, ri, 0:3, :] = low.astype(jnp.float32)[5:8]
            grown[z, ri, 3:19, :] = middle.astype(jnp.float32)
            grown[z, ri, 19:22, :] = high.astype(jnp.float32)[0:3]

    def deep(z):
        return ((z >= 0) & (z < NZ)).astype(jnp.float32)

    good_rows = in_grid(lax.broadcasted_iota(jnp.int32, (24, 1), 0) + (16 * coil - 3))

    def widen(z, _):
        keep = good_rows * deep(z + 4 * slab - 3)
        both = [shifted(grown[z, ri] * keep) for ri in range(2)]
        wide_0[z] = jnp.concatenate([both[ri][dx] for dx in range(3) for ri in range(2)], axis=0).astype(jnp.bfloat16)
        return 0

    lax.fori_loop(0, 10, widen, 0, unroll=2)

    def layer_1(z, _):
        hidden = jnp.dot(matrix_1[:, :432], padded_rows(wide_0, z), preferred_element_type=jnp.float32)
        wide_1[z] = (jnp.maximum(hidden, 0.0) * deep(z + 4 * slab - 2)).astype(jnp.bfloat16)
        return 0

    lax.fori_loop(0, 8, layer_1, 0)

    def summed(taps, rows):
        return (
            pltpu.roll(taps[:rows], 1, 1) * not_first
            + taps[rows : 2 * rows]
            + pltpu.roll(taps[2 * rows :], 255, 1) * not_last
        )

    def layer_2(z, _):
        window = wide_1[pl.ds(z, 3)].reshape(960, 256)
        taps = jnp.dot(matrix_2[:, :960], window, preferred_element_type=jnp.float32)
        hidden = jnp.maximum(summed(taps, 288), 0.0) * deep(z + 4 * slab - 1)
        wide_2[z] = hidden.astype(jnp.bfloat16)
        return 0

    lax.fori_loop(0, 6, layer_2, 0)

    for z in range(4):
        window = wide_2[z : z + 3].reshape(864, 256)
        taps = jnp.dot(matrix_3[:, :864], window, preferred_element_type=jnp.float32)
        total = summed(taps, 32)
        for ri in range(2):
            refined_out[ri, z] = block[64 * ri + 16 * z : 64 * ri + 16 * z + 16, :] + total[16 * ri : 16 * ri + 16]

    arrived(a_rcv.reshape(256, 8, 128), 3, 255)
    tmp[...] = a_rcv[...].astype(jnp.float32)
    rows = lax.broadcasted_iota(jnp.int32, (128, 128), 0)
    columns = lax.broadcasted_iota(jnp.int32, (128, 128), 1)
    keep = lax.dot_general(
        (rows == columns).astype(jnp.float32), mask, (((1,), (1,)), ((), ())), preferred_element_type=jnp.float32
    )
    for k in range(4):
        parts = [tmp[:, :, 4 * ri + k, :].reshape(256, 128).T.astype(jnp.bfloat16) for ri in range(2)]
        found = jnp.concatenate(parts, axis=1)
        found = jnp.dot(found, x_h[...], preferred_element_type=jnp.float32) + jnp.dot(
            found, x_l[...], preferred_element_type=jnp.float32
        )
        here = keep[:, k : k + 1]
        residual_out[0, 0, :, k, :] = here * (found[:, :256] - kspace[0, 0, :, k, :])
        residual_out[1, 0, :, k, :] = here * (found[:, 256:] - kspace[1, 0, :, k, :])
    left(i_msg, 0, 31)
    left(s_msg.reshape(256, 8, 128), 1, 255)
    left(y_msg.reshape(256, 8, 128), 2, 255)
    left(a_msg.reshape(256, 8, 128), 3, 255)
    left(c_msg.reshape(256, 1, 128), 4, 255)


OPERANDS = (
    ((2, 4, 128, 256), jnp.float32),
    ((2, 1, 4, 128, 256), jnp.float32),
    ((2, 1, 128, 4, 256), jnp.float32),
    ((4, 128), jnp.int32),
    ((16, 2, 27), jnp.bfloat16),
    ((16, 16, 27), jnp.bfloat16),
    ((2, 16, 27), jnp.bfloat16),
) + (((256, 256), jnp.bfloat16),) * 8 + (((512, 512), jnp.bfloat16),) * 2


def unrolled_step(image, sensitivity, kspace, sampled, w_in, w_mid, w_out):
    operands = (image, sensitivity, kspace, sampled.T) + tuple(
        w.transpose(1, 2, 0) for w in (w_in, w_mid, w_out)
    )
    operands += tuple(jnp.asarray(m) for m in constants())
    whole = pl.BlockSpec(memory_space=pltpu.VMEM)
    message = (32, 8, 8, 128)
    vmem = pltpu.VMEM
    return pl.pallas_call(
        unrolled_kernel,
        out_shape=(
            jax.ShapeDtypeStruct((2, 4, 16, 256), jnp.float32),
            jax.ShapeDtypeStruct((2, 1, 128, 4, 256), jnp.float32),
        ),
        in_specs=[pl.BlockSpec(memory_space=pltpu.HBM)] * len(operands),
        out_specs=(whole, whole),
        scratch_shapes=[vmem(shape, dtype) for shape, dtype in OPERANDS]
        + [pltpu.SemaphoreType.DMA((len(OPERANDS),))]
        + [vmem(message, jnp.int16), vmem(message, jnp.int16)]
        + [vmem((32, 2, 8, 128), jnp.int16), vmem((32, 2, 8, 128), jnp.int16)]
        + [vmem(message, jnp.int16), vmem(message, jnp.int16)]
        + [vmem(message, jnp.bfloat16), vmem(message, jnp.bfloat16)]
        + [vmem((32, 8, 1, 128), jnp.float32), vmem((32, 8, 1, 128), jnp.float32)]
        + [
            vmem(message, jnp.float32),
            vmem((8, 256, 128), jnp.float32),
            vmem((8, 256, 128), jnp.float32),
            vmem((4, 256, 256), jnp.float32),
            vmem((256, 128), jnp.float32),
            vmem((2, 3, 2, 16, 256), jnp.bfloat16),
            vmem((2, 3, 2, 16, 256), jnp.bfloat16),
            vmem((2, 4, 2, 8, 256), jnp.bfloat16),
            vmem((2, 4, 2, 8, 256), jnp.bfloat16),
            vmem((2, 2, 3, 2, 8, 256), jnp.bfloat16),
            vmem((2, 2, 3, 2, 8, 256), jnp.bfloat16),
            vmem((128, 256), jnp.float32),
            vmem((10, 2, 24, 256), jnp.float32),
            vmem((10, 144, 256), jnp.bfloat16),
            vmem((8, 320, 256), jnp.bfloat16),
            vmem((6, 288, 256), jnp.bfloat16),
            vmem((4, 320, 128), jnp.float32),
            vmem((7, 8, 16, 128), jnp.float32),
            vmem((320, 512), jnp.bfloat16),
            vmem((864, 1024), jnp.bfloat16),
            vmem((96, 896), jnp.bfloat16),
            vmem((8, 896), jnp.float32),
            pltpu.SemaphoreType.DMA((5,)),
            pltpu.SemaphoreType.DMA((5,)),
            pltpu.SemaphoreType.DMA((8,)),
            pltpu.SemaphoreType.DMA((8,)),
        ],
        compiler_params=pltpu.CompilerParams(
            collective_id=0, has_side_effects=True, vmem_limit_bytes=52 * 1024 * 1024
        ),
        name="unrolled_step",
    )(*(pltpu.with_memory_space_constraint(x, pltpu.HBM) for x in operands))


def solution(mesh):
    placed = (
        P(None, "slab", None, None),
        P(None, "coil", "slab", None, None),
        P(None, "coil", None, "slab", None),
        P(None, "slab"),
        P(),
        P(),
        P(),
    )
    return jax.shard_map(
        unrolled_step,
        mesh=mesh,
        in_specs=placed,
        out_specs=(P(None, "slab", "coil", None), P(None, "coil", None, "slab", None)),
        check_vma=False,
    )
```

```python
import functools
import math

import jax
import jax.numpy as jnp
import ml_dtypes
import numpy as np
from jax import lax
from jax.experimental import pallas as pl
from jax.experimental.pallas import tpu as pltpu
from jax.sharding import PartitionSpec as P

NX = 256
NY = 128
NZ = 128

step_size = 0.5
SENS_CODE = 16383.0
IMAGE_CODE = 5461.0
DATA_CODE = 3970.0
MESH = pl.DeviceIdType.MESH


def halves(matrix):
    high = matrix.astype(ml_dtypes.bfloat16)
    low = (matrix - high.astype(np.float64)).astype(ml_dtypes.bfloat16)
    return high, low


def blocks(length, inverse):
    positions = np.arange(length)
    angles = (positions[:, None] * positions[None, :] % length) * (2.0 * math.pi / length)
    cosines = np.cos(angles) / math.sqrt(length)
    sines = np.sin(angles) / math.sqrt(length)
    if inverse:
        sines = -sines
    return np.block([[cosines, sines], [-sines, cosines]])


def mixed_rows(matrix):
    return matrix.reshape(2, 32, 4, -1).transpose(1, 0, 2, 3).reshape(256, -1)


def constants():
    forward = blocks(128, False)
    backward = blocks(128, True)
    made = []
    for matrix in (
        mixed_rows(forward.T).T,
        mixed_rows(forward),
        mixed_rows(backward.T).T,
        mixed_rows(backward),
        blocks(256, True),
    ):
        made.extend(halves(matrix))
    return made


def product(pair, data):
    high = data.astype(jnp.bfloat16)
    low = (data - high.astype(jnp.float32)).astype(jnp.bfloat16)
    first, second = (pair[0][...], pair[1][...])
    dot = functools.partial(jnp.dot, preferred_element_type=jnp.float32)
    return dot(first, high) + (dot(first, low) + dot(second, high))


def product_nt(pair, data):
    high = data.astype(jnp.bfloat16)
    low = (data - high.astype(jnp.float32)).astype(jnp.bfloat16)
    first, second = (pair[0][...], pair[1][...])

    def dot(a, b):
        return lax.dot_general(a, b, (((1,), (1,)), ((), ())), preferred_element_type=jnp.float32)

    return dot(first, high) + (dot(first, low) + dot(second, high))


def regrouped(x):
    parts = []
    for k in range(2):
        lanes = slice(128 * k, 128 * k + 128)
        parts.append(jnp.concatenate([x[:128, lanes], x[128:, lanes]], axis=1))
    return jnp.concatenate(parts, axis=0)


def swapped(x):
    return pltpu.roll(x.reshape(32, 8, 128), 4, 1).reshape(256, 128)


def coded(x, scale):
    return jnp.round(x * scale).astype(jnp.int32).astype(jnp.int16)


def companded(x):
    size = jnp.sqrt(jnp.abs(x)) * DATA_CODE
    return jnp.round(jnp.where(x < 0, -size, size)).astype(jnp.int32).astype(jnp.int16)


def decoded(x):
    return x.astype(jnp.int32).astype(jnp.float32)


def wrapped(value, size):
    return jnp.where(value >= size, value - size, value)


def padded_rows(ref, z):
    return ref[pl.ds(z, 3)].reshape(432, 256)


def unrolled_kernel(*refs):
    count = len(OPERANDS)
    held = refs[count + 2 : 2 * count + 2]
    load_sem = refs[2 * count + 2]
    loads = [pltpu.make_async_copy(refs[k], held[k], load_sem.at[k]) for k in range(count)]
    for load in loads:
        load.start()
    image, sens, kspace, sampled, w_in, w_mid, w_out = held[:7]
    g1f_h, g1f_l, g2f_h, g2f_l, g1i_h, g1i_l, g2i_h, g2i_l, x_h, x_l = held[7:]
    refined_out, residual_out = refs[count : count + 2]
    (
        s_msg, s_rcv, i_msg, i_rcv, y_msg, y_rcv, a_msg, a_rcv, c_msg, c_rcv,
        tmp, sens_a, sens_b, spec, cur,
        zh_msg, zh_rcv, yh_msg, yh_rcv, ch_msg, ch_rcv,
        block, grown, wide_0, wide_1, wide_2, toeplitz_1, toeplitz_3, matrix_1, matrix_2, matrix_3, base_3,
        send_sem, recv_sem, halo_send, halo_recv,
    ) = refs[2 * count + 3 :]
    slab = lax.axis_index("slab")
    coil = lax.axis_index("coil")
    g1f, g2f, g1i, g2i, gx = ((g1f_h, g1f_l), (g2f_h, g2f_l), (g1i_h, g1i_l), (g2i_h, g2i_l), (x_h, x_l))

    coils = [wrapped(coil + k, 8) for k in (4, 5, 3, 2, 6, 7, 1, 0)]

    def every_other(act, first=0, last=16):
        def rings(k, _):
            step = (k + 1) // 2 * (2 * lax.rem(k, 2) - 1)
            for s in (wrapped(slab + 8 + step, 32), wrapped(slab + 24 + step, 32)):
                for c in coils:
                    act(s, c)
            return 0

        lax.fori_loop(first, min(last, 15), rings, 0)
        if last == 16:
            for c in coils:
                act(wrapped(slab + 16, 32), c)
            for c in coils[:7]:
                act(slab, c)

    barrier = pltpu.get_barrier_semaphore()
    every_other(
        lambda s, c: pl.semaphore_signal(barrier, inc=1, device_id={"slab": s, "coil": c}, device_id_type=MESH)
    )

    def arrived(flat, which, count):
        part = flat.at[pl.ds(0, count)]
        pltpu.make_async_copy(part, part, recv_sem.at[which]).wait()

    def left(flat, which, count):
        part = flat.at[pl.ds(0, count)]
        pltpu.make_async_copy(part, part, send_sem.at[which]).wait()

    def send_all(msg, rcv, which, first=0, last=16):
        every_other(
            lambda s, c: pltpu.make_async_remote_copy(
                msg.at[s, c], rcv.at[slab, coil], send_sem.at[which], recv_sem.at[which],
                device_id={"slab": s, "coil": c}, device_id_type=MESH,
            ).start(),
            first,
            last,
        )
        if last == 16:
            rcv[slab, coil] = msg[slab, coil]

    loads[1].wait()
    for ri in range(2):
        for z in range(4):
            tmp[:, :, ri * 4 + z, :] = sens[ri, 0, z].T.reshape(32, 8, 128)
    s_msg[...] = coded(tmp[...], SENS_CODE)
    loads[0].wait()
    loads[3].wait()
    for ri in range(2):
        for z in range(4):
            tmp[:, :, ri * 4 + z, :] = image[ri, z].T.reshape(32, 8, 128)
    mask = sampled[...].astype(jnp.float32)
    mask = jnp.concatenate([mask, mask], axis=0)
    own = coded(tmp[:, coil], IMAGE_CODE)
    i_msg[:, 0] = own
    i_msg[:, 1] = jnp.broadcast_to(coded(mask, 1.0)[None], (32, 8, 128))

    for number in (2, *range(4, count)):
        loads[number].wait()
    tap = lax.broadcasted_iota(jnp.int32, (27, 1024), 0)
    lane = lax.broadcasted_iota(jnp.int32, (27, 1024), 1)
    tap_z, tap_y, tap_x = (tap // 9, lax.rem(tap // 3, 3), lax.rem(tap, 3))

    def placed(taps, spot):
        here = (lane == spot).astype(jnp.float32)[:, : 128 * spot_parts]
        return jnp.dot(taps, here, preferred_element_type=jnp.float32)

    def in_grid(y):
        return ((y >= 0) & (y < NY)).astype(jnp.float32)

    taps_1, taps_2, taps_3 = (w[...].astype(jnp.float32) for w in (w_in, w_mid, w_out))
    spot_parts = 4
    base_1 = sum(placed(taps_1[:, ri, :], 144 * tap_z + 24 * (2 * tap_x + ri) + tap_y) for ri in range(2))
    good = in_grid(lax.broadcasted_iota(jnp.int32, (24, 1), 0) + (16 * coil - 2))
    for o in range(16):
        spread = jnp.broadcast_to(base_1[o : o + 1, :], (24, 512))
        turned = pltpu.roll(spread, 0, 1, stride=1, stride_axis=0) * good
        for part in range(4):
            toeplitz_1[part, pl.ds(o, 20, stride=16), :] = turned[:20, 128 * part : 128 * part + 128]
    for part in range(4):
        matrix_1[:, 128 * part : 128 * part + 128] = toeplitz_1[part].astype(jnp.bfloat16)
    spot_parts = 8
    for dx in range(3):
        base_2 = sum(
            placed(taps_2[:, i, :], jnp.where(tap_x == dx, 320 * tap_z + 16 * tap_y + i, -1)) for i in range(16)
        )
        for y in range(18):
            turned = pltpu.roll(base_2, 16 * y, 1) if y else base_2
            first = 288 * dx + 16 * y
            matrix_2[first : first + 16, :] = (turned * in_grid(16 * coil - 1 + y)).astype(jnp.bfloat16)
    spot_parts = 7
    for dx in range(3):
        base_3[2 * dx : 2 * dx + 2, :] = sum(
            placed(taps_3[:, i, :], jnp.where(tap_x == dx, 288 * tap_z + 16 * tap_y + i, -1)) for i in range(16)
        )
    base_3[6:8, :] = jnp.zeros((2, 896), jnp.float32)
    for y in range(16):
        turned = pltpu.roll(base_3[...], 16 * y, 1) if y else base_3[...]
        for part in range(7):
            toeplitz_3[part, :, y, :] = turned[:, 128 * part : 128 * part + 128]
    for part in range(7):
        matrix_3[:, 128 * part : 128 * part + 128] = toeplitz_3[part, 0:6].reshape(96, 128).astype(jnp.bfloat16)
    grown[...] = jnp.zeros((10, 2, 24, 256), jnp.float32)

    pl.semaphore_wait(barrier, 255)

    def send_image(k, _):
        s = wrapped(slab + k, 32)
        pltpu.make_async_remote_copy(
            i_msg.at[s], i_rcv.at[slab], send_sem.at[0], recv_sem.at[0],
            device_id={"slab": s, "coil": coil}, device_id_type=MESH,
        ).start()
        return 0

    lax.fori_loop(1, 32, send_image, 0)
    i_rcv[slab] = i_msg[slab]
    send_all(s_msg, s_rcv, 1)

    stacked = jnp.concatenate(
        [jnp.concatenate([kspace[0, 0, :, k, :], kspace[1, 0, :, k, :]], axis=1) for k in range(4)], axis=0
    )
    hybrid = product_nt(gx, stacked)
    for ri in range(2):
        for k in range(4):
            tmp[:, :, ri * 4 + k, :] = hybrid[256 * ri : 256 * ri + 256, 128 * k : 128 * k + 128].reshape(32, 8, 128)
    y_msg[...] = companded(tmp[...])
    send_all(y_msg, y_rcv, 2)

    arrived(i_rcv, 0, 31)
    arrived(s_rcv.reshape(256, 8, 128), 1, 255)
    cur[...] = decoded(i_rcv[:, 0]).reshape(256, 128) * (1.0 / IMAGE_CODE)

    lower = lax.broadcasted_iota(jnp.int32, (256, 128), 0) % 8 < 4

    def unpack(c, _):
        both = decoded(s_rcv[:, c]).reshape(256, 128) * (1.0 / SENS_CODE)
        other = swapped(both)
        sens_a[c] = jnp.where(lower, both, other)
        sens_b[c] = jnp.where(lower, -other, both)
        return 0

    lax.fori_loop(0, 8, unpack, 0)

    def forward(p, now, turned):
        c = 2 * p
        v = jnp.concatenate(
            [sens_a[c] * now + sens_b[c] * turned, sens_a[c + 1] * now + sens_b[c + 1] * turned], axis=1
        )
        return product_nt(g2f, regrouped(product(g1f, v)))

    def backward(p, found, weight):
        c = 2 * p
        res = []
        for k in range(2):
            code = decoded(y_rcv[:, c + k]).reshape(256, 128)
            data = code * jnp.abs(code) * (1.0 / DATA_CODE**2)
            res.append(weight * (found[:, 128 * k : 128 * k + 128] - data))
        b = product_nt(g2i, regrouped(product(g1i, jnp.concatenate(res, axis=1))))
        total = None
        for k in range(2):
            part = b[:, 128 * k : 128 * k + 128]
            term = sens_a[c + k] * part - sens_b[c + k] * swapped(part)
            total = term if total is None else total + term
        return total

    now = cur[...]
    turned = swapped(now)

    def ahead(p, _):
        spec[p] = forward(p, now, turned)
        return 0

    lax.fori_loop(0, 4, ahead, 0, unroll=2)
    arrived(y_rcv.reshape(256, 8, 128), 2, 255)
    weight = decoded(i_rcv[:, 1]).reshape(256, 128)

    def add_back(p, g):
        return g + backward(p, spec[p], weight)

    grad = lax.fori_loop(0, 4, add_back, jnp.zeros((256, 128), jnp.float32), unroll=4)
    now_1 = now - step_size * grad
    turned_1 = swapped(now_1)

    def again(p, _):
        found = forward(p, now_1, turned_1)
        for k in range(2):
            a_msg[:, 2 * p + k] = found[:, 128 * k : 128 * k + 128].reshape(32, 8, 128).astype(jnp.bfloat16)
        spec[p] = found
        return 0

    lax.fori_loop(0, 4, again, 0, unroll=4)
    send_all(a_msg, a_rcv, 3, 0, 3)
    grad = lax.fori_loop(0, 4, add_back, jnp.zeros((256, 128), jnp.float32), unroll=4)
    cur[...] = now_1 - step_size * grad

    lane_block = lax.broadcasted_iota(jnp.int32, (32, 128), 1) // 16
    picked = [cur[pl.ds(r, 32, stride=8), :] for r in range(8)]
    for c in range(8):
        packed = None
        for r in range(8):
            shift = 16 * ((r - c) % 8)
            moved = pltpu.roll(picked[r], shift, 1) if shift else picked[r]
            packed = moved if packed is None else jnp.where(lane_block == r, moved, packed)
        c_msg[:, c, 0, :] = packed
    send_all(c_msg, c_rcv, 4)
    send_all(a_msg, a_rcv, 3, 3, 16)
    arrived(c_rcv.reshape(256, 1, 128), 4, 255)
    block[...] = c_rcv[:, :, 0, :].reshape(256, 128).T

    starts = [[block[64 * ri + 16 * z : 64 * ri + 16 * z + 16, :] for ri in range(2)] for z in range(4)]
    for z in range(4):
        for ri in range(2):
            first = starts[z][ri][:8].astype(jnp.bfloat16)
            last = starts[z][ri][8:].astype(jnp.bfloat16)
            yh_msg[0, z, ri] = first
            yh_msg[1, z, ri] = last
            for side in range(2):
                if 0 <= z - side < 3:
                    zh_msg[side, z - side, ri] = starts[z][ri].astype(jnp.bfloat16)
                    ch_msg[side, 0, z - side, ri] = first
                    ch_msg[side, 1, z - side, ri] = last

    halos = []
    for side in range(2):
        s = lax.rem(slab + (31 if side == 0 else 1), 32)
        c = lax.rem(coil + (7 if side == 0 else 1), 8)
        halos.append((zh_msg.at[side], zh_rcv.at[1 - side], s, coil))
        halos.append((yh_msg.at[side], yh_rcv.at[1 - side], slab, c))
        for other in range(2):
            c = lax.rem(coil + (7 if other == 0 else 1), 8)
            halos.append((ch_msg.at[side, other], ch_rcv.at[1 - side, 1 - other], s, c))
    halos = [
        pltpu.make_async_remote_copy(
            src, dst, halo_send.at[k], halo_recv.at[k], device_id={"slab": s, "coil": c}, device_id_type=MESH
        )
        for k, (src, dst, s, c) in enumerate(halos)
    ]
    for halo in halos:
        halo.start()
    for halo in halos:
        halo.wait()

    lane_x = lax.broadcasted_iota(jnp.int32, (1, 256), 1)
    not_first = (lane_x > 0).astype(jnp.float32)
    not_last = (lane_x < 255).astype(jnp.float32)

    def shifted(x):
        return [pltpu.roll(x, 1, 1) * not_first, x, pltpu.roll(x, 255, 1) * not_last]

    for z in range(10):
        for ri in range(2):
            if z < 3:
                middle, low, high = (zh_rcv[0, z, ri], ch_rcv[0, 0, z, ri], ch_rcv[0, 1, z, ri])
            elif z < 7:
                middle, low, high = (starts[z - 3][ri], yh_rcv[0, z - 3, ri], yh_rcv[1, z - 3, ri])
            else:
                middle, low, high = (zh_rcv[1, z - 7, ri], ch_rcv[1, 0, z - 7, ri], ch_rcv[1, 1, z - 7, ri])
            grown[z, ri, 0:3, :] = low.astype(jnp.float32)[5:8]
            grown[z, ri, 3:19, :] = middle.astype(jnp.float32)
            grown[z, ri, 19:22, :] = high.astype(jnp.float32)[0:3]

    def deep(z):
        return ((z >= 0) & (z < NZ)).astype(jnp.float32)

    good_rows = in_grid(lax.broadcasted_iota(jnp.int32, (24, 1), 0) + (16 * coil - 3))

    def widen(z, _):
        keep = good_rows * deep(z + 4 * slab - 3)
        both = [shifted(grown[z, ri] * keep) for ri in range(2)]
        wide_0[z] = jnp.concatenate([both[ri][dx] for dx in range(3) for ri in range(2)], axis=0).astype(jnp.bfloat16)
        return 0

    lax.fori_loop(0, 10, widen, 0, unroll=2)

    def layer_1(z, _):
        hidden = jnp.dot(matrix_1[:, :432], padded_rows(wide_0, z), preferred_element_type=jnp.float32)
        wide_1[z] = (jnp.maximum(hidden, 0.0) * deep(z + 4 * slab - 2)).astype(jnp.bfloat16)
        return 0

    lax.fori_loop(0, 8, layer_1, 0, unroll=2)

    def summed(taps, rows):
        return (
            pltpu.roll(taps[:rows], 1, 1) * not_first
            + taps[rows : 2 * rows]
            + pltpu.roll(taps[2 * rows :], 255, 1) * not_last
        )

    def layer_2(z, _):
        window = wide_1[pl.ds(z, 3)].reshape(960, 256)
        taps = jnp.dot(matrix_2[:, :960], window, preferred_element_type=jnp.float32)
        hidden = jnp.maximum(summed(taps, 288), 0.0) * deep(z + 4 * slab - 1)
        wide_2[z] = hidden.astype(jnp.bfloat16)
        return 0

    lax.fori_loop(0, 6, layer_2, 0, unroll=2)

    for z in range(4):
        window = wide_2[z : z + 3].reshape(864, 256)
        taps = jnp.dot(matrix_3[:, :864], window, preferred_element_type=jnp.float32)
        total = summed(taps, 32)
        for ri in range(2):
            refined_out[ri, z] = block[64 * ri + 16 * z : 64 * ri + 16 * z + 16, :] + total[16 * ri : 16 * ri + 16]

    arrived(a_rcv.reshape(256, 8, 128), 3, 255)
    tmp[...] = a_rcv[...].astype(jnp.float32)
    rows = lax.broadcasted_iota(jnp.int32, (128, 128), 0)
    columns = lax.broadcasted_iota(jnp.int32, (128, 128), 1)
    keep = lax.dot_general(
        (rows == columns).astype(jnp.float32), mask, (((1,), (1,)), ((), ())), preferred_element_type=jnp.float32
    )
    for k in range(4):
        parts = [tmp[:, :, 4 * ri + k, :].reshape(256, 128).T.astype(jnp.bfloat16) for ri in range(2)]
        found = jnp.concatenate(parts, axis=1)
        found = jnp.dot(found, x_h[...], preferred_element_type=jnp.float32) + jnp.dot(
            found, x_l[...], preferred_element_type=jnp.float32
        )
        here = keep[:, k : k + 1]
        residual_out[0, 0, :, k, :] = here * (found[:, :256] - kspace[0, 0, :, k, :])
        residual_out[1, 0, :, k, :] = here * (found[:, 256:] - kspace[1, 0, :, k, :])
    left(i_msg, 0, 31)
    left(s_msg.reshape(256, 8, 128), 1, 255)
    left(y_msg.reshape(256, 8, 128), 2, 255)
    left(a_msg.reshape(256, 8, 128), 3, 255)
    left(c_msg.reshape(256, 1, 128), 4, 255)


OPERANDS = (
    ((2, 4, 128, 256), jnp.float32),
    ((2, 1, 4, 128, 256), jnp.float32),
    ((2, 1, 128, 4, 256), jnp.float32),
    ((4, 128), jnp.int32),
    ((16, 2, 27), jnp.bfloat16),
    ((16, 16, 27), jnp.bfloat16),
    ((2, 16, 27), jnp.bfloat16),
) + (((256, 256), jnp.bfloat16),) * 8 + (((512, 512), jnp.bfloat16),) * 2


def unrolled_step(image, sensitivity, kspace, sampled, w_in, w_mid, w_out):
    operands = (image, sensitivity, kspace, sampled.T) + tuple(
        w.transpose(1, 2, 0) for w in (w_in, w_mid, w_out)
    )
    operands += tuple(jnp.asarray(m) for m in constants())
    whole = pl.BlockSpec(memory_space=pltpu.VMEM)
    message = (32, 8, 8, 128)
    vmem = pltpu.VMEM
    return pl.pallas_call(
        unrolled_kernel,
        out_shape=(
            jax.ShapeDtypeStruct((2, 4, 16, 256), jnp.float32),
            jax.ShapeDtypeStruct((2, 1, 128, 4, 256), jnp.float32),
        ),
        in_specs=[pl.BlockSpec(memory_space=pltpu.HBM)] * len(operands),
        out_specs=(whole, whole),
        scratch_shapes=[vmem(shape, dtype) for shape, dtype in OPERANDS]
        + [pltpu.SemaphoreType.DMA((len(OPERANDS),))]
        + [vmem(message, jnp.int16), vmem(message, jnp.int16)]
        + [vmem((32, 2, 8, 128), jnp.int16), vmem((32, 2, 8, 128), jnp.int16)]
        + [vmem(message, jnp.int16), vmem(message, jnp.int16)]
        + [vmem(message, jnp.bfloat16), vmem(message, jnp.bfloat16)]
        + [vmem((32, 8, 1, 128), jnp.float32), vmem((32, 8, 1, 128), jnp.float32)]
        + [
            vmem(message, jnp.float32),
            vmem((8, 256, 128), jnp.float32),
            vmem((8, 256, 128), jnp.float32),
            vmem((4, 256, 256), jnp.float32),
            vmem((256, 128), jnp.float32),
            vmem((2, 3, 2, 16, 256), jnp.bfloat16),
            vmem((2, 3, 2, 16, 256), jnp.bfloat16),
            vmem((2, 4, 2, 8, 256), jnp.bfloat16),
            vmem((2, 4, 2, 8, 256), jnp.bfloat16),
            vmem((2, 2, 3, 2, 8, 256), jnp.bfloat16),
            vmem((2, 2, 3, 2, 8, 256), jnp.bfloat16),
            vmem((128, 256), jnp.float32),
            vmem((10, 2, 24, 256), jnp.float32),
            vmem((10, 144, 256), jnp.bfloat16),
            vmem((8, 320, 256), jnp.bfloat16),
            vmem((6, 288, 256), jnp.bfloat16),
            vmem((4, 320, 128), jnp.float32),
            vmem((7, 8, 16, 128), jnp.float32),
            vmem((320, 512), jnp.bfloat16),
            vmem((864, 1024), jnp.bfloat16),
            vmem((96, 896), jnp.bfloat16),
            vmem((8, 896), jnp.float32),
            pltpu.SemaphoreType.DMA((5,)),
            pltpu.SemaphoreType.DMA((5,)),
            pltpu.SemaphoreType.DMA((8,)),
            pltpu.SemaphoreType.DMA((8,)),
        ],
        compiler_params=pltpu.CompilerParams(
            collective_id=0, has_side_effects=True, vmem_limit_bytes=52 * 1024 * 1024
        ),
        name="unrolled_step",
    )(*(pltpu.with_memory_space_constraint(x, pltpu.HBM) for x in operands))


def solution(mesh):
    placed = (
        P(None, "slab", None, None),
        P(None, "coil", "slab", None, None),
        P(None, "coil", None, "slab", None),
        P(None, "slab"),
        P(),
        P(),
        P(),
    )
    return jax.shard_map(
        unrolled_step,
        mesh=mesh,
        in_specs=placed,
        out_specs=(P(None, "slab", "coil", None), P(None, "coil", None, "slab", None)),
        check_vma=False,
    )
```

```python
import functools
import math

import jax
import jax.numpy as jnp
import ml_dtypes
import numpy as np
from jax import lax
from jax.experimental import pallas as pl
from jax.experimental.pallas import tpu as pltpu
from jax.sharding import PartitionSpec as P

NX = 256
NY = 128
NZ = 128

step_size = 0.5
SENS_CODE = 16383.0
IMAGE_CODE = 5461.0
DATA_CODE = 3970.0
MESH = pl.DeviceIdType.MESH


def halves(matrix):
    high = matrix.astype(ml_dtypes.bfloat16)
    low = (matrix - high.astype(np.float64)).astype(ml_dtypes.bfloat16)
    return high, low


def blocks(length, inverse):
    positions = np.arange(length)
    angles = (positions[:, None] * positions[None, :] % length) * (2.0 * math.pi / length)
    cosines = np.cos(angles) / math.sqrt(length)
    sines = np.sin(angles) / math.sqrt(length)
    if inverse:
        sines = -sines
    return np.block([[cosines, sines], [-sines, cosines]])


def mixed_rows(matrix):
    return matrix.reshape(2, 32, 4, -1).transpose(1, 0, 2, 3).reshape(256, -1)


def constants():
    forward = blocks(128, False)
    backward = blocks(128, True)
    made = []
    for matrix in (
        mixed_rows(forward.T).T,
        mixed_rows(forward),
        mixed_rows(backward.T).T,
        mixed_rows(backward),
        blocks(256, True),
    ):
        made.extend(halves(matrix))
    return made


def product(pair, data):
    high = data.astype(jnp.bfloat16)
    low = (data - high.astype(jnp.float32)).astype(jnp.bfloat16)
    first, second = (pair[0][...], pair[1][...])
    dot = functools.partial(jnp.dot, preferred_element_type=jnp.float32)
    return dot(first, high) + (dot(first, low) + dot(second, high))


def product_nt(pair, data):
    high = data.astype(jnp.bfloat16)
    low = (data - high.astype(jnp.float32)).astype(jnp.bfloat16)
    first, second = (pair[0][...], pair[1][...])

    def dot(a, b):
        return lax.dot_general(a, b, (((1,), (1,)), ((), ())), preferred_element_type=jnp.float32)

    return dot(first, high) + (dot(first, low) + dot(second, high))


def regrouped(x):
    parts = []
    for k in range(2):
        lanes = slice(128 * k, 128 * k + 128)
        parts.append(jnp.concatenate([x[:128, lanes], x[128:, lanes]], axis=1))
    return jnp.concatenate(parts, axis=0)


def swapped(x):
    return pltpu.roll(x.reshape(32, 8, 128), 4, 1).reshape(256, 128)


def coded(x, scale):
    return jnp.round(x * scale).astype(jnp.int32).astype(jnp.int16)


def companded(x):
    size = jnp.sqrt(jnp.abs(x)) * DATA_CODE
    return jnp.round(jnp.where(x < 0, -size, size)).astype(jnp.int32).astype(jnp.int16)


def decoded(x):
    return x.astype(jnp.int32).astype(jnp.float32)


def wrapped(value, size):
    return jnp.where(value >= size, value - size, value)


def padded_rows(ref, z):
    return ref[pl.ds(z, 3)].reshape(432, 256)


def unrolled_kernel(*refs):
    count = len(OPERANDS)
    held = refs[count + 2 : 2 * count + 2]
    load_sem = refs[2 * count + 2]
    loads = [pltpu.make_async_copy(refs[k], held[k], load_sem.at[k]) for k in range(count)]
    for load in loads:
        load.start()
    image, sens, kspace, sampled, w_in, w_mid, w_out = held[:7]
    g1f_h, g1f_l, g2f_h, g2f_l, g1i_h, g1i_l, g2i_h, g2i_l, x_h, x_l = held[7:]
    refined_out, residual_out = refs[count : count + 2]
    (
        s_msg, s_rcv, i_msg, i_rcv, y_msg, y_rcv, a_msg, a_rcv, c_msg, c_rcv,
        tmp, sens_a, sens_b, spec, cur,
        zh_msg, zh_rcv, yh_msg, yh_rcv, ch_msg, ch_rcv,
        block, grown, wide_0, wide_1, wide_2, toeplitz_1, toeplitz_3, matrix_1, matrix_2, matrix_3, base_3,
        send_sem, recv_sem, halo_send, halo_recv,
    ) = refs[2 * count + 3 :]
    slab = lax.axis_index("slab")
    coil = lax.axis_index("coil")
    g1f, g2f, g1i, g2i, gx = ((g1f_h, g1f_l), (g2f_h, g2f_l), (g1i_h, g1i_l), (g2i_h, g2i_l), (x_h, x_l))

    coils = [wrapped(coil + k, 8) for k in (4, 5, 3, 2, 6, 7, 1, 0)]

    def every_other(act, first=0, last=16):
        def rings(k, _):
            step = (k + 1) // 2 * (2 * lax.rem(k, 2) - 1)
            for s in (wrapped(slab + 8 + step, 32), wrapped(slab + 24 + step, 32)):
                for c in coils:
                    act(s, c)
            return 0

        lax.fori_loop(first, min(last, 15), rings, 0)
        if last == 16:
            for c in coils:
                act(wrapped(slab + 16, 32), c)
            for c in coils[:7]:
                act(slab, c)

    barrier = pltpu.get_barrier_semaphore()
    every_other(
        lambda s, c: pl.semaphore_signal(barrier, inc=1, device_id={"slab": s, "coil": c}, device_id_type=MESH)
    )

    def arrived(flat, which, count):
        part = flat.at[pl.ds(0, count)]
        pltpu.make_async_copy(part, part, recv_sem.at[which]).wait()

    def left(flat, which, count):
        part = flat.at[pl.ds(0, count)]
        pltpu.make_async_copy(part, part, send_sem.at[which]).wait()

    def send_all(msg, rcv, which, first=0, last=16):
        every_other(
            lambda s, c: pltpu.make_async_remote_copy(
                msg.at[s, c], rcv.at[slab, coil], send_sem.at[which], recv_sem.at[which],
                device_id={"slab": s, "coil": c}, device_id_type=MESH,
            ).start(),
            first,
            last,
        )
        if last == 16:
            rcv[slab, coil] = msg[slab, coil]

    loads[1].wait()
    for ri in range(2):
        for z in range(4):
            tmp[:, :, ri * 4 + z, :] = sens[ri, 0, z].T.reshape(32, 8, 128)
    s_msg[...] = coded(tmp[...], SENS_CODE)
    loads[0].wait()
    loads[3].wait()
    for ri in range(2):
        for z in range(4):
            tmp[:, :, ri * 4 + z, :] = image[ri, z].T.reshape(32, 8, 128)
    mask = sampled[...].astype(jnp.float32)
    mask = jnp.concatenate([mask, mask], axis=0)
    own = coded(tmp[:, coil], IMAGE_CODE)
    i_msg[:, 0] = own
    i_msg[:, 1] = jnp.broadcast_to(coded(mask, 1.0)[None], (32, 8, 128))

    for number in (2, *range(4, count)):
        loads[number].wait()
    tap = lax.broadcasted_iota(jnp.int32, (27, 1024), 0)
    lane = lax.broadcasted_iota(jnp.int32, (27, 1024), 1)
    tap_z, tap_y, tap_x = (tap // 9, lax.rem(tap // 3, 3), lax.rem(tap, 3))

    def placed(taps, spot):
        here = (lane == spot).astype(jnp.float32)[:, : 128 * spot_parts]
        return jnp.dot(taps, here, preferred_element_type=jnp.float32)

    def in_grid(y):
        return ((y >= 0) & (y < NY)).astype(jnp.float32)

    taps_1, taps_2, taps_3 = (w[...].astype(jnp.float32) for w in (w_in, w_mid, w_out))
    spot_parts = 4
    base_1 = sum(placed(taps_1[:, ri, :], 144 * tap_z + 24 * (2 * tap_x + ri) + tap_y) for ri in range(2))
    good = in_grid(lax.broadcasted_iota(jnp.int32, (24, 1), 0) + (16 * coil - 2))
    for o in range(16):
        spread = jnp.broadcast_to(base_1[o : o + 1, :], (24, 512))
        turned = pltpu.roll(spread, 0, 1, stride=1, stride_axis=0) * good
        for part in range(4):
            toeplitz_1[part, pl.ds(o, 20, stride=16), :] = turned[:20, 128 * part : 128 * part + 128]
    for part in range(4):
        matrix_1[:, 128 * part : 128 * part + 128] = toeplitz_1[part].astype(jnp.bfloat16)
    spot_parts = 8
    for dx in range(3):
        base_2 = sum(
            placed(taps_2[:, i, :], jnp.where(tap_x == dx, 320 * tap_z + 16 * tap_y + i, -1)) for i in range(16)
        )
        for y in range(18):
            turned = pltpu.roll(base_2, 16 * y, 1) if y else base_2
            first = 288 * dx + 16 * y
            matrix_2[first : first + 16, :] = (turned * in_grid(16 * coil - 1 + y)).astype(jnp.bfloat16)
    spot_parts = 7
    for dx in range(3):
        base_3[2 * dx : 2 * dx + 2, :] = sum(
            placed(taps_3[:, i, :], jnp.where(tap_x == dx, 288 * tap_z + 16 * tap_y + i, -1)) for i in range(16)
        )
    base_3[6:8, :] = jnp.zeros((2, 896), jnp.float32)
    for y in range(16):
        turned = pltpu.roll(base_3[...], 16 * y, 1) if y else base_3[...]
        for part in range(7):
            toeplitz_3[part, :, y, :] = turned[:, 128 * part : 128 * part + 128]
    for part in range(7):
        matrix_3[:, 128 * part : 128 * part + 128] = toeplitz_3[part, 0:6].reshape(96, 128).astype(jnp.bfloat16)
    grown[...] = jnp.zeros((10, 2, 24, 256), jnp.float32)

    pl.semaphore_wait(barrier, 255)

    def send_image(k, _):
        s = wrapped(slab + k, 32)
        pltpu.make_async_remote_copy(
            i_msg.at[s], i_rcv.at[slab], send_sem.at[0], recv_sem.at[0],
            device_id={"slab": s, "coil": coil}, device_id_type=MESH,
        ).start()
        return 0

    lax.fori_loop(1, 32, send_image, 0)
    i_rcv[slab] = i_msg[slab]
    send_all(s_msg, s_rcv, 1)

    stacked = jnp.concatenate(
        [jnp.concatenate([kspace[0, 0, :, k, :], kspace[1, 0, :, k, :]], axis=1) for k in range(4)], axis=0
    )
    hybrid = product_nt(gx, stacked)
    for ri in range(2):
        for k in range(4):
            tmp[:, :, ri * 4 + k, :] = hybrid[256 * ri : 256 * ri + 256, 128 * k : 128 * k + 128].reshape(32, 8, 128)
    y_msg[...] = companded(tmp[...])
    send_all(y_msg, y_rcv, 2)

    arrived(i_rcv, 0, 31)
    arrived(s_rcv.reshape(256, 8, 128), 1, 255)
    cur[...] = decoded(i_rcv[:, 0]).reshape(256, 128) * (1.0 / IMAGE_CODE)

    lower = lax.broadcasted_iota(jnp.int32, (256, 128), 0) % 8 < 4

    def unpack(c, _):
        both = decoded(s_rcv[:, c]).reshape(256, 128) * (1.0 / SENS_CODE)
        other = swapped(both)
        sens_a[c] = jnp.where(lower, both, other)
        sens_b[c] = jnp.where(lower, -other, both)
        return 0

    lax.fori_loop(0, 8, unpack, 0)

    def forward(p, now, turned):
        c = 2 * p
        v = jnp.concatenate(
            [sens_a[c] * now + sens_b[c] * turned, sens_a[c + 1] * now + sens_b[c + 1] * turned], axis=1
        )
        return product_nt(g2f, regrouped(product(g1f, v)))

    def backward(p, found, weight):
        c = 2 * p
        res = []
        for k in range(2):
            code = decoded(y_rcv[:, c + k]).reshape(256, 128)
            data = code * jnp.abs(code) * (1.0 / DATA_CODE**2)
            res.append(weight * (found[:, 128 * k : 128 * k + 128] - data))
        b = product_nt(g2i, regrouped(product(g1i, jnp.concatenate(res, axis=1))))
        total = None
        for k in range(2):
            part = b[:, 128 * k : 128 * k + 128]
            term = sens_a[c + k] * part - sens_b[c + k] * swapped(part)
            total = term if total is None else total + term
        return total

    now = cur[...]
    turned = swapped(now)

    def ahead(p, _):
        spec[p] = forward(p, now, turned)
        return 0

    lax.fori_loop(0, 4, ahead, 0, unroll=2)
    arrived(y_rcv.reshape(256, 8, 128), 2, 255)
    weight = decoded(i_rcv[:, 1]).reshape(256, 128)

    def add_back(p, g):
        return g + backward(p, spec[p], weight)

    grad = lax.fori_loop(0, 4, add_back, jnp.zeros((256, 128), jnp.float32), unroll=4)
    now_1 = now - step_size * grad
    turned_1 = swapped(now_1)

    def again(p, _):
        found = forward(p, now_1, turned_1)
        for k in range(2):
            a_msg[:, 2 * p + k] = found[:, 128 * k : 128 * k + 128].reshape(32, 8, 128).astype(jnp.bfloat16)
        spec[p] = found
        return 0

    lax.fori_loop(0, 4, again, 0, unroll=4)
    send_all(a_msg, a_rcv, 3, 0, 3)
    grad = lax.fori_loop(0, 4, add_back, jnp.zeros((256, 128), jnp.float32), unroll=4)
    cur[...] = now_1 - step_size * grad

    lane_block = lax.broadcasted_iota(jnp.int32, (32, 128), 1) // 16
    picked = [cur[pl.ds(r, 32, stride=8), :] for r in range(8)]
    for c in range(8):
        packed = None
        for r in range(8):
            shift = 16 * ((r - c) % 8)
            moved = pltpu.roll(picked[r], shift, 1) if shift else picked[r]
            packed = moved if packed is None else jnp.where(lane_block == r, moved, packed)
        c_msg[:, c, 0, :] = packed
    send_all(c_msg, c_rcv, 4)
    send_all(a_msg, a_rcv, 3, 3, 16)
    arrived(c_rcv.reshape(256, 1, 128), 4, 255)
    block[...] = c_rcv[:, :, 0, :].reshape(256, 128).T

    starts = [[block[64 * ri + 16 * z : 64 * ri + 16 * z + 16, :] for ri in range(2)] for z in range(4)]
    for z in range(4):
        for ri in range(2):
            first = starts[z][ri][:8].astype(jnp.bfloat16)
            last = starts[z][ri][8:].astype(jnp.bfloat16)
            yh_msg[0, z, ri] = first
            yh_msg[1, z, ri] = last
            for side in range(2):
                if 0 <= z - side < 3:
                    zh_msg[side, z - side, ri] = starts[z][ri].astype(jnp.bfloat16)
                    ch_msg[side, 0, z - side, ri] = first
                    ch_msg[side, 1, z - side, ri] = last

    halos = []
    for side in range(2):
        s = lax.rem(slab + (31 if side == 0 else 1), 32)
        c = lax.rem(coil + (7 if side == 0 else 1), 8)
        halos.append((zh_msg.at[side], zh_rcv.at[1 - side], s, coil))
        halos.append((yh_msg.at[side], yh_rcv.at[1 - side], slab, c))
        for other in range(2):
            c = lax.rem(coil + (7 if other == 0 else 1), 8)
            halos.append((ch_msg.at[side, other], ch_rcv.at[1 - side, 1 - other], s, c))
    halos = [
        pltpu.make_async_remote_copy(
            src, dst, halo_send.at[k], halo_recv.at[k], device_id={"slab": s, "coil": c}, device_id_type=MESH
        )
        for k, (src, dst, s, c) in enumerate(halos)
    ]
    for halo in halos:
        halo.start()
    for halo in halos:
        halo.wait()

    lane_x = lax.broadcasted_iota(jnp.int32, (1, 256), 1)
    not_first = (lane_x > 0).astype(jnp.float32)
    not_last = (lane_x < 255).astype(jnp.float32)

    def shifted(x):
        return [pltpu.roll(x, 1, 1) * not_first, x, pltpu.roll(x, 255, 1) * not_last]

    for z in range(10):
        for ri in range(2):
            if z < 3:
                middle, low, high = (zh_rcv[0, z, ri], ch_rcv[0, 0, z, ri], ch_rcv[0, 1, z, ri])
            elif z < 7:
                middle, low, high = (starts[z - 3][ri], yh_rcv[0, z - 3, ri], yh_rcv[1, z - 3, ri])
            else:
                middle, low, high = (zh_rcv[1, z - 7, ri], ch_rcv[1, 0, z - 7, ri], ch_rcv[1, 1, z - 7, ri])
            grown[z, ri, 0:3, :] = low.astype(jnp.float32)[5:8]
            grown[z, ri, 3:19, :] = middle.astype(jnp.float32)
            grown[z, ri, 19:22, :] = high.astype(jnp.float32)[0:3]

    def deep(z):
        return ((z >= 0) & (z < NZ)).astype(jnp.float32)

    good_rows = in_grid(lax.broadcasted_iota(jnp.int32, (24, 1), 0) + (16 * coil - 3))

    def widen(z, _):
        keep = good_rows * deep(z + 4 * slab - 3)
        both = [shifted(grown[z, ri] * keep) for ri in range(2)]
        wide_0[z] = jnp.concatenate([both[ri][dx] for dx in range(3) for ri in range(2)], axis=0).astype(jnp.bfloat16)
        return 0

    lax.fori_loop(0, 10, widen, 0, unroll=2)

    def layer_1(z, _):
        hidden = jnp.dot(matrix_1[:, :432], padded_rows(wide_0, z), preferred_element_type=jnp.float32)
        wide_1[z] = (jnp.maximum(hidden, 0.0) * deep(z + 4 * slab - 2)).astype(jnp.bfloat16)
        return 0

    lax.fori_loop(0, 8, layer_1, 0, unroll=4)

    def summed(taps, rows):
        return (
            pltpu.roll(taps[:rows], 1, 1) * not_first
            + taps[rows : 2 * rows]
            + pltpu.roll(taps[2 * rows :], 255, 1) * not_last
        )

    def layer_2(z, _):
        window = wide_1[pl.ds(z, 3)].reshape(960, 256)
        taps = jnp.dot(matrix_2[:, :960], window, preferred_element_type=jnp.float32)
        hidden = jnp.maximum(summed(taps, 288), 0.0) * deep(z + 4 * slab - 1)
        wide_2[z] = hidden.astype(jnp.bfloat16)
        return 0

    lax.fori_loop(0, 6, layer_2, 0, unroll=3)

    for z in range(4):
        window = wide_2[z : z + 3].reshape(864, 256)
        taps = jnp.dot(matrix_3[:, :864], window, preferred_element_type=jnp.float32)
        total = summed(taps, 32)
        for ri in range(2):
            refined_out[ri, z] = block[64 * ri + 16 * z : 64 * ri + 16 * z + 16, :] + total[16 * ri : 16 * ri + 16]

    arrived(a_rcv.reshape(256, 8, 128), 3, 255)
    tmp[...] = a_rcv[...].astype(jnp.float32)
    rows = lax.broadcasted_iota(jnp.int32, (128, 128), 0)
    columns = lax.broadcasted_iota(jnp.int32, (128, 128), 1)
    keep = lax.dot_general(
        (rows == columns).astype(jnp.float32), mask, (((1,), (1,)), ((), ())), preferred_element_type=jnp.float32
    )
    parts = [
        jnp.concatenate(
            [tmp[:, :, 4 * ri + k, :].reshape(256, 128).T.astype(jnp.bfloat16) for ri in range(2)], axis=1
        )
        for k in range(4)
    ]
    parts = jnp.concatenate(parts, axis=0)
    found = jnp.dot(parts, x_h[...], preferred_element_type=jnp.float32) + jnp.dot(
        parts, x_l[...], preferred_element_type=jnp.float32
    )
    for k in range(4):
        here = keep[:, k : k + 1]
        rows = slice(128 * k, 128 * k + 128)
        residual_out[0, 0, :, k, :] = here * (found[rows, :256] - kspace[0, 0, :, k, :])
        residual_out[1, 0, :, k, :] = here * (found[rows, 256:] - kspace[1, 0, :, k, :])
    left(i_msg, 0, 31)
    left(s_msg.reshape(256, 8, 128), 1, 255)
    left(y_msg.reshape(256, 8, 128), 2, 255)
    left(a_msg.reshape(256, 8, 128), 3, 255)
    left(c_msg.reshape(256, 1, 128), 4, 255)


OPERANDS = (
    ((2, 4, 128, 256), jnp.float32),
    ((2, 1, 4, 128, 256), jnp.float32),
    ((2, 1, 128, 4, 256), jnp.float32),
    ((4, 128), jnp.int32),
    ((16, 2, 27), jnp.bfloat16),
    ((16, 16, 27), jnp.bfloat16),
    ((2, 16, 27), jnp.bfloat16),
) + (((256, 256), jnp.bfloat16),) * 8 + (((512, 512), jnp.bfloat16),) * 2


def unrolled_step(image, sensitivity, kspace, sampled, w_in, w_mid, w_out):
    operands = (image, sensitivity, kspace, sampled.T) + tuple(
        w.transpose(1, 2, 0) for w in (w_in, w_mid, w_out)
    )
    operands += tuple(jnp.asarray(m) for m in constants())
    whole = pl.BlockSpec(memory_space=pltpu.VMEM)
    message = (32, 8, 8, 128)
    vmem = pltpu.VMEM
    return pl.pallas_call(
        unrolled_kernel,
        out_shape=(
            jax.ShapeDtypeStruct((2, 4, 16, 256), jnp.float32),
            jax.ShapeDtypeStruct((2, 1, 128, 4, 256), jnp.float32),
        ),
        in_specs=[pl.BlockSpec(memory_space=pltpu.HBM)] * len(operands),
        out_specs=(whole, whole),
        scratch_shapes=[vmem(shape, dtype) for shape, dtype in OPERANDS]
        + [pltpu.SemaphoreType.DMA((len(OPERANDS),))]
        + [vmem(message, jnp.int16), vmem(message, jnp.int16)]
        + [vmem((32, 2, 8, 128), jnp.int16), vmem((32, 2, 8, 128), jnp.int16)]
        + [vmem(message, jnp.int16), vmem(message, jnp.int16)]
        + [vmem(message, jnp.bfloat16), vmem(message, jnp.bfloat16)]
        + [vmem((32, 8, 1, 128), jnp.float32), vmem((32, 8, 1, 128), jnp.float32)]
        + [
            vmem(message, jnp.float32),
            vmem((8, 256, 128), jnp.float32),
            vmem((8, 256, 128), jnp.float32),
            vmem((4, 256, 256), jnp.float32),
            vmem((256, 128), jnp.float32),
            vmem((2, 3, 2, 16, 256), jnp.bfloat16),
            vmem((2, 3, 2, 16, 256), jnp.bfloat16),
            vmem((2, 4, 2, 8, 256), jnp.bfloat16),
            vmem((2, 4, 2, 8, 256), jnp.bfloat16),
            vmem((2, 2, 3, 2, 8, 256), jnp.bfloat16),
            vmem((2, 2, 3, 2, 8, 256), jnp.bfloat16),
            vmem((128, 256), jnp.float32),
            vmem((10, 2, 24, 256), jnp.float32),
            vmem((10, 144, 256), jnp.bfloat16),
            vmem((8, 320, 256), jnp.bfloat16),
            vmem((6, 288, 256), jnp.bfloat16),
            vmem((4, 320, 128), jnp.float32),
            vmem((7, 8, 16, 128), jnp.float32),
            vmem((320, 512), jnp.bfloat16),
            vmem((864, 1024), jnp.bfloat16),
            vmem((96, 896), jnp.bfloat16),
            vmem((8, 896), jnp.float32),
            pltpu.SemaphoreType.DMA((5,)),
            pltpu.SemaphoreType.DMA((5,)),
            pltpu.SemaphoreType.DMA((8,)),
            pltpu.SemaphoreType.DMA((8,)),
        ],
        compiler_params=pltpu.CompilerParams(
            collective_id=0, has_side_effects=True, vmem_limit_bytes=52 * 1024 * 1024
        ),
        name="unrolled_step",
    )(*(pltpu.with_memory_space_constraint(x, pltpu.HBM) for x in operands))


def solution(mesh):
    placed = (
        P(None, "slab", None, None),
        P(None, "coil", "slab", None, None),
        P(None, "coil", None, "slab", None),
        P(None, "slab"),
        P(),
        P(),
        P(),
    )
    return jax.shard_map(
        unrolled_step,
        mesh=mesh,
        in_specs=placed,
        out_specs=(P(None, "slab", "coil", None), P(None, "coil", None, "slab", None)),
        check_vma=False,
    )
```

```python
import functools
import math

import jax
import jax.numpy as jnp
import ml_dtypes
import numpy as np
from jax import lax
from jax.experimental import pallas as pl
from jax.experimental.pallas import tpu as pltpu
from jax.sharding import PartitionSpec as P

NX = 256
NY = 128
NZ = 128

step_size = 0.5
SENS_CODE = 16383.0
IMAGE_CODE = 5461.0
DATA_CODE = 3970.0
MESH = pl.DeviceIdType.MESH


def halves(matrix):
    high = matrix.astype(ml_dtypes.bfloat16)
    low = (matrix - high.astype(np.float64)).astype(ml_dtypes.bfloat16)
    return high, low


def blocks(length, inverse):
    positions = np.arange(length)
    angles = (positions[:, None] * positions[None, :] % length) * (2.0 * math.pi / length)
    cosines = np.cos(angles) / math.sqrt(length)
    sines = np.sin(angles) / math.sqrt(length)
    if inverse:
        sines = -sines
    return np.block([[cosines, sines], [-sines, cosines]])


def mixed_rows(matrix):
    return matrix.reshape(2, 32, 4, -1).transpose(1, 0, 2, 3).reshape(256, -1)


def constants():
    forward = blocks(128, False)
    backward = blocks(128, True)
    made = []
    for matrix in (
        mixed_rows(forward.T).T,
        mixed_rows(forward),
        mixed_rows(backward.T).T,
        mixed_rows(backward),
        blocks(256, True),
    ):
        made.extend(halves(matrix))
    return made


def product(pair, data):
    high = data.astype(jnp.bfloat16)
    low = (data - high.astype(jnp.float32)).astype(jnp.bfloat16)
    first, second = (pair[0][...], pair[1][...])
    dot = functools.partial(jnp.dot, preferred_element_type=jnp.float32)
    return dot(first, high) + (dot(first, low) + dot(second, high))


def product_nt(pair, data):
    high = data.astype(jnp.bfloat16)
    low = (data - high.astype(jnp.float32)).astype(jnp.bfloat16)
    first, second = (pair[0][...], pair[1][...])

    def dot(a, b):
        return lax.dot_general(a, b, (((1,), (1,)), ((), ())), preferred_element_type=jnp.float32)

    return dot(first, high) + (dot(first, low) + dot(second, high))


def regrouped(x):
    parts = []
    for k in range(2):
        lanes = slice(128 * k, 128 * k + 128)
        parts.append(jnp.concatenate([x[:128, lanes], x[128:, lanes]], axis=1))
    return jnp.concatenate(parts, axis=0)


def swapped(x):
    return pltpu.roll(x.reshape(32, 8, 128), 4, 1).reshape(256, 128)


def coded(x, scale):
    return jnp.round(x * scale).astype(jnp.int32).astype(jnp.int16)


def companded(x):
    size = jnp.sqrt(jnp.abs(x)) * DATA_CODE
    return jnp.round(jnp.where(x < 0, -size, size)).astype(jnp.int32).astype(jnp.int16)


def decoded(x):
    return x.astype(jnp.int32).astype(jnp.float32)


def wrapped(value, size):
    return jnp.where(value >= size, value - size, value)


def padded_rows(ref, z):
    return ref[pl.ds(z, 3)].reshape(432, 256)


def unrolled_kernel(*refs):
    count = len(OPERANDS)
    held = refs[count + 2 : 2 * count + 2]
    load_sem = refs[2 * count + 2]
    loads = [pltpu.make_async_copy(refs[k], held[k], load_sem.at[k]) for k in range(count)]
    for load in loads:
        load.start()
    image, sens, kspace, sampled, w_in, w_mid, w_out = held[:7]
    g1f_h, g1f_l, g2f_h, g2f_l, g1i_h, g1i_l, g2i_h, g2i_l, x_h, x_l = held[7:]
    refined_out, residual_out = refs[count : count + 2]
    (
        s_msg, s_rcv, i_msg, i_rcv, y_msg, y_rcv, a_msg, a_rcv, c_msg, c_rcv,
        tmp, sens_a, sens_b, spec, cur,
        zh_msg, zh_rcv, yh_msg, yh_rcv, ch_msg, ch_rcv,
        block, grown, wide_0, wide_1, wide_2, toeplitz_1, toeplitz_3, matrix_1, matrix_2, matrix_3, base_3,
        send_sem, recv_sem, halo_send, halo_recv,
    ) = refs[2 * count + 3 :]
    slab = lax.axis_index("slab")
    coil = lax.axis_index("coil")
    g1f, g2f, g1i, g2i, gx = ((g1f_h, g1f_l), (g2f_h, g2f_l), (g1i_h, g1i_l), (g2i_h, g2i_l), (x_h, x_l))

    coils = [wrapped(coil + k, 8) for k in (4, 5, 3, 2, 6, 7, 1, 0)]

    def every_other(act, first=0, last=16):
        def rings(k, _):
            step = (k + 1) // 2 * (2 * lax.rem(k, 2) - 1)
            for s in (wrapped(slab + 8 + step, 32), wrapped(slab + 24 + step, 32)):
                for c in coils:
                    act(s, c)
            return 0

        lax.fori_loop(first, min(last, 15), rings, 0)
        if last == 16:
            for c in coils:
                act(wrapped(slab + 16, 32), c)
            for c in coils[:7]:
                act(slab, c)

    barrier = pltpu.get_barrier_semaphore()
    every_other(
        lambda s, c: pl.semaphore_signal(barrier, inc=1, device_id={"slab": s, "coil": c}, device_id_type=MESH)
    )

    def arrived(flat, which, count):
        part = flat.at[pl.ds(0, count)]
        pltpu.make_async_copy(part, part, recv_sem.at[which]).wait()

    def left(flat, which, count):
        part = flat.at[pl.ds(0, count)]
        pltpu.make_async_copy(part, part, send_sem.at[which]).wait()

    def send_all(msg, rcv, which, first=0, last=16):
        every_other(
            lambda s, c: pltpu.make_async_remote_copy(
                msg.at[s, c], rcv.at[slab, coil], send_sem.at[which], recv_sem.at[which],
                device_id={"slab": s, "coil": c}, device_id_type=MESH,
            ).start(),
            first,
            last,
        )
        if last == 16:
            rcv[slab, coil] = msg[slab, coil]

    loads[1].wait()
    for ri in range(2):
        for z in range(4):
            tmp[:, :, ri * 4 + z, :] = sens[ri, 0, z].T.reshape(32, 8, 128)
    s_msg[...] = coded(tmp[...], SENS_CODE)
    loads[0].wait()
    loads[3].wait()
    for ri in range(2):
        for z in range(4):
            tmp[:, :, ri * 4 + z, :] = image[ri, z].T.reshape(32, 8, 128)
    mask = sampled[...].astype(jnp.float32)
    mask = jnp.concatenate([mask, mask], axis=0)
    own = coded(tmp[:, coil], IMAGE_CODE)
    i_msg[:, 0] = own
    i_msg[:, 1] = jnp.broadcast_to(coded(mask, 1.0)[None], (32, 8, 128))

    for number in (2, *range(4, count)):
        loads[number].wait()
    tap = lax.broadcasted_iota(jnp.int32, (27, 1024), 0)
    lane = lax.broadcasted_iota(jnp.int32, (27, 1024), 1)
    tap_z, tap_y, tap_x = (tap // 9, lax.rem(tap // 3, 3), lax.rem(tap, 3))

    def placed(taps, spot):
        here = (lane == spot).astype(jnp.float32)[:, : 128 * spot_parts]
        return jnp.dot(taps, here, preferred_element_type=jnp.float32)

    def in_grid(y):
        return ((y >= 0) & (y < NY)).astype(jnp.float32)

    taps_1, taps_2, taps_3 = (w[...].astype(jnp.float32) for w in (w_in, w_mid, w_out))
    spot_parts = 4
    base_1 = sum(placed(taps_1[:, ri, :], 144 * tap_z + 24 * (2 * tap_x + ri) + tap_y) for ri in range(2))
    good = in_grid(lax.broadcasted_iota(jnp.int32, (24, 1), 0) + (16 * coil - 2))
    for o in range(16):
        spread = jnp.broadcast_to(base_1[o : o + 1, :], (24, 512))
        turned = pltpu.roll(spread, 0, 1, stride=1, stride_axis=0) * good
        for part in range(4):
            toeplitz_1[part, pl.ds(o, 20, stride=16), :] = turned[:20, 128 * part : 128 * part + 128]
    for part in range(4):
        matrix_1[:, 128 * part : 128 * part + 128] = toeplitz_1[part].astype(jnp.bfloat16)
    spot_parts = 8
    for dx in range(3):
        base_2 = sum(
            placed(taps_2[:, i, :], jnp.where(tap_x == dx, 320 * tap_z + 16 * tap_y + i, -1)) for i in range(16)
        )
        for y in range(18):
            turned = pltpu.roll(base_2, 16 * y, 1) if y else base_2
            first = 288 * dx + 16 * y
            matrix_2[first : first + 16, :] = (turned * in_grid(16 * coil - 1 + y)).astype(jnp.bfloat16)
    spot_parts = 7
    for dx in range(3):
        base_3[2 * dx : 2 * dx + 2, :] = sum(
            placed(taps_3[:, i, :], jnp.where(tap_x == dx, 288 * tap_z + 16 * tap_y + i, -1)) for i in range(16)
        )
    base_3[6:8, :] = jnp.zeros((2, 896), jnp.float32)
    for y in range(16):
        turned = pltpu.roll(base_3[...], 16 * y, 1) if y else base_3[...]
        for part in range(7):
            toeplitz_3[part, :, y, :] = turned[:, 128 * part : 128 * part + 128]
    for part in range(7):
        matrix_3[:, 128 * part : 128 * part + 128] = toeplitz_3[part, 0:6].reshape(96, 128).astype(jnp.bfloat16)
    grown[...] = jnp.zeros((10, 2, 24, 256), jnp.float32)

    pl.semaphore_wait(barrier, 255)

    def send_image(k, _):
        s = wrapped(slab + k, 32)
        pltpu.make_async_remote_copy(
            i_msg.at[s], i_rcv.at[slab], send_sem.at[0], recv_sem.at[0],
            device_id={"slab": s, "coil": coil}, device_id_type=MESH,
        ).start()
        return 0

    lax.fori_loop(1, 32, send_image, 0)
    i_rcv[slab] = i_msg[slab]
    send_all(s_msg, s_rcv, 1)

    stacked = jnp.concatenate(
        [jnp.concatenate([kspace[0, 0, :, k, :], kspace[1, 0, :, k, :]], axis=1) for k in range(4)], axis=0
    )
    hybrid = product_nt(gx, stacked)
    for ri in range(2):
        for k in range(4):
            tmp[:, :, ri * 4 + k, :] = hybrid[256 * ri : 256 * ri + 256, 128 * k : 128 * k + 128].reshape(32, 8, 128)
    y_msg[...] = companded(tmp[...])
    send_all(y_msg, y_rcv, 2)

    arrived(i_rcv, 0, 31)
    arrived(s_rcv.reshape(256, 8, 128), 1, 255)
    cur[...] = decoded(i_rcv[:, 0]).reshape(256, 128) * (1.0 / IMAGE_CODE)

    lower = lax.broadcasted_iota(jnp.int32, (256, 128), 0) % 8 < 4

    def unpack(c, _):
        both = decoded(s_rcv[:, c]).reshape(256, 128) * (1.0 / SENS_CODE)
        other = swapped(both)
        sens_a[c] = jnp.where(lower, both, other)
        sens_b[c] = jnp.where(lower, -other, both)
        return 0

    lax.fori_loop(0, 8, unpack, 0, unroll=4)

    def forward(p, now, turned):
        c = 2 * p
        v = jnp.concatenate(
            [sens_a[c] * now + sens_b[c] * turned, sens_a[c + 1] * now + sens_b[c + 1] * turned], axis=1
        )
        return product_nt(g2f, regrouped(product(g1f, v)))

    def backward(p, found, weight):
        c = 2 * p
        res = []
        for k in range(2):
            code = decoded(y_rcv[:, c + k]).reshape(256, 128)
            data = code * jnp.abs(code) * (1.0 / DATA_CODE**2)
            res.append(weight * (found[:, 128 * k : 128 * k + 128] - data))
        b = product_nt(g2i, regrouped(product(g1i, jnp.concatenate(res, axis=1))))
        total = None
        for k in range(2):
            part = b[:, 128 * k : 128 * k + 128]
            term = sens_a[c + k] * part - sens_b[c + k] * swapped(part)
            total = term if total is None else total + term
        return total

    now = cur[...]
    turned = swapped(now)

    def ahead(p, _):
        spec[p] = forward(p, now, turned)
        return 0

    lax.fori_loop(0, 4, ahead, 0, unroll=2)
    arrived(y_rcv.reshape(256, 8, 128), 2, 255)
    weight = decoded(i_rcv[:, 1]).reshape(256, 128)

    def add_back(p, g):
        return g + backward(p, spec[p], weight)

    grad = lax.fori_loop(0, 4, add_back, jnp.zeros((256, 128), jnp.float32), unroll=4)
    now_1 = now - step_size * grad
    turned_1 = swapped(now_1)

    def again(p, _):
        found = forward(p, now_1, turned_1)
        for k in range(2):
            a_msg[:, 2 * p + k] = found[:, 128 * k : 128 * k + 128].reshape(32, 8, 128).astype(jnp.bfloat16)
        spec[p] = found
        return 0

    lax.fori_loop(0, 4, again, 0, unroll=4)
    send_all(a_msg, a_rcv, 3, 0, 3)
    grad = lax.fori_loop(0, 4, add_back, jnp.zeros((256, 128), jnp.float32), unroll=4)
    cur[...] = now_1 - step_size * grad

    lane_block = lax.broadcasted_iota(jnp.int32, (32, 128), 1) // 16
    picked = [cur[pl.ds(r, 32, stride=8), :] for r in range(8)]
    for c in range(8):
        packed = None
        for r in range(8):
            shift = 16 * ((r - c) % 8)
            moved = pltpu.roll(picked[r], shift, 1) if shift else picked[r]
            packed = moved if packed is None else jnp.where(lane_block == r, moved, packed)
        c_msg[:, c, 0, :] = packed
    send_all(c_msg, c_rcv, 4)
    send_all(a_msg, a_rcv, 3, 3, 16)
    arrived(c_rcv.reshape(256, 1, 128), 4, 255)
    block[...] = c_rcv[:, :, 0, :].reshape(256, 128).T

    starts = [[block[64 * ri + 16 * z : 64 * ri + 16 * z + 16, :] for ri in range(2)] for z in range(4)]
    for z in range(4):
        for ri in range(2):
            first = starts[z][ri][:8].astype(jnp.bfloat16)
            last = starts[z][ri][8:].astype(jnp.bfloat16)
            yh_msg[0, z, ri] = first
            yh_msg[1, z, ri] = last
            for side in range(2):
                if 0 <= z - side < 3:
                    zh_msg[side, z - side, ri] = starts[z][ri].astype(jnp.bfloat16)
                    ch_msg[side, 0, z - side, ri] = first
                    ch_msg[side, 1, z - side, ri] = last

    halos = []
    for side in range(2):
        s = lax.rem(slab + (31 if side == 0 else 1), 32)
        c = lax.rem(coil + (7 if side == 0 else 1), 8)
        halos.append((zh_msg.at[side], zh_rcv.at[1 - side], s, coil))
        halos.append((yh_msg.at[side], yh_rcv.at[1 - side], slab, c))
        for other in range(2):
            c = lax.rem(coil + (7 if other == 0 else 1), 8)
            halos.append((ch_msg.at[side, other], ch_rcv.at[1 - side, 1 - other], s, c))
    halos = [
        pltpu.make_async_remote_copy(
            src, dst, halo_send.at[k], halo_recv.at[k], device_id={"slab": s, "coil": c}, device_id_type=MESH
        )
        for k, (src, dst, s, c) in enumerate(halos)
    ]
    for halo in halos:
        halo.start()
    for halo in halos:
        halo.wait()

    lane_x = lax.broadcasted_iota(jnp.int32, (1, 256), 1)
    not_first = (lane_x > 0).astype(jnp.float32)
    not_last = (lane_x < 255).astype(jnp.float32)

    def shifted(x):
        return [pltpu.roll(x, 1, 1) * not_first, x, pltpu.roll(x, 255, 1) * not_last]

    for z in range(10):
        for ri in range(2):
            if z < 3:
                middle, low, high = (zh_rcv[0, z, ri], ch_rcv[0, 0, z, ri], ch_rcv[0, 1, z, ri])
            elif z < 7:
                middle, low, high = (starts[z - 3][ri], yh_rcv[0, z - 3, ri], yh_rcv[1, z - 3, ri])
            else:
                middle, low, high = (zh_rcv[1, z - 7, ri], ch_rcv[1, 0, z - 7, ri], ch_rcv[1, 1, z - 7, ri])
            grown[z, ri, 0:3, :] = low.astype(jnp.float32)[5:8]
            grown[z, ri, 3:19, :] = middle.astype(jnp.float32)
            grown[z, ri, 19:22, :] = high.astype(jnp.float32)[0:3]

    def deep(z):
        return ((z >= 0) & (z < NZ)).astype(jnp.float32)

    good_rows = in_grid(lax.broadcasted_iota(jnp.int32, (24, 1), 0) + (16 * coil - 3))

    def widen(z, _):
        keep = good_rows * deep(z + 4 * slab - 3)
        both = [shifted(grown[z, ri] * keep) for ri in range(2)]
        wide_0[z] = jnp.concatenate([both[ri][dx] for dx in range(3) for ri in range(2)], axis=0).astype(jnp.bfloat16)
        return 0

    lax.fori_loop(0, 10, widen, 0, unroll=5)

    def layer_1(z, _):
        hidden = jnp.dot(matrix_1[:, :432], padded_rows(wide_0, z), preferred_element_type=jnp.float32)
        wide_1[z] = (jnp.maximum(hidden, 0.0) * deep(z + 4 * slab - 2)).astype(jnp.bfloat16)
        return 0

    lax.fori_loop(0, 8, layer_1, 0, unroll=4)

    def summed(taps, rows):
        return (
            pltpu.roll(taps[:rows], 1, 1) * not_first
            + taps[rows : 2 * rows]
            + pltpu.roll(taps[2 * rows :], 255, 1) * not_last
        )

    def layer_2(z, _):
        window = wide_1[pl.ds(z, 3)].reshape(960, 256)
        taps = jnp.dot(matrix_2[:, :960], window, preferred_element_type=jnp.float32)
        hidden = jnp.maximum(summed(taps, 288), 0.0) * deep(z + 4 * slab - 1)
        wide_2[z] = hidden.astype(jnp.bfloat16)
        return 0

    lax.fori_loop(0, 6, layer_2, 0, unroll=3)

    for z in range(4):
        window = wide_2[z : z + 3].reshape(864, 256)
        taps = jnp.dot(matrix_3[:, :864], window, preferred_element_type=jnp.float32)
        total = summed(taps, 32)
        for ri in range(2):
            refined_out[ri, z] = block[64 * ri + 16 * z : 64 * ri + 16 * z + 16, :] + total[16 * ri : 16 * ri + 16]

    arrived(a_rcv.reshape(256, 8, 128), 3, 255)
    tmp[...] = a_rcv[...].astype(jnp.float32)
    rows = lax.broadcasted_iota(jnp.int32, (128, 128), 0)
    columns = lax.broadcasted_iota(jnp.int32, (128, 128), 1)
    keep = lax.dot_general(
        (rows == columns).astype(jnp.float32), mask, (((1,), (1,)), ((), ())), preferred_element_type=jnp.float32
    )
    parts = [
        jnp.concatenate(
            [tmp[:, :, 4 * ri + k, :].reshape(256, 128).T.astype(jnp.bfloat16) for ri in range(2)], axis=1
        )
        for k in range(4)
    ]
    parts = jnp.concatenate(parts, axis=0)
    found = jnp.dot(parts, x_h[...], preferred_element_type=jnp.float32) + jnp.dot(
        parts, x_l[...], preferred_element_type=jnp.float32
    )
    for k in range(4):
        here = keep[:, k : k + 1]
        rows = slice(128 * k, 128 * k + 128)
        residual_out[0, 0, :, k, :] = here * (found[rows, :256] - kspace[0, 0, :, k, :])
        residual_out[1, 0, :, k, :] = here * (found[rows, 256:] - kspace[1, 0, :, k, :])
    left(i_msg, 0, 31)
    left(s_msg.reshape(256, 8, 128), 1, 255)
    left(y_msg.reshape(256, 8, 128), 2, 255)
    left(a_msg.reshape(256, 8, 128), 3, 255)
    left(c_msg.reshape(256, 1, 128), 4, 255)


OPERANDS = (
    ((2, 4, 128, 256), jnp.float32),
    ((2, 1, 4, 128, 256), jnp.float32),
    ((2, 1, 128, 4, 256), jnp.float32),
    ((4, 128), jnp.int32),
    ((16, 2, 27), jnp.bfloat16),
    ((16, 16, 27), jnp.bfloat16),
    ((2, 16, 27), jnp.bfloat16),
) + (((256, 256), jnp.bfloat16),) * 8 + (((512, 512), jnp.bfloat16),) * 2


def unrolled_step(image, sensitivity, kspace, sampled, w_in, w_mid, w_out):
    operands = (image, sensitivity, kspace, sampled.T) + tuple(
        w.transpose(1, 2, 0) for w in (w_in, w_mid, w_out)
    )
    operands += tuple(jnp.asarray(m) for m in constants())
    whole = pl.BlockSpec(memory_space=pltpu.VMEM)
    message = (32, 8, 8, 128)
    vmem = pltpu.VMEM
    return pl.pallas_call(
        unrolled_kernel,
        out_shape=(
            jax.ShapeDtypeStruct((2, 4, 16, 256), jnp.float32),
            jax.ShapeDtypeStruct((2, 1, 128, 4, 256), jnp.float32),
        ),
        in_specs=[pl.BlockSpec(memory_space=pltpu.HBM)] * len(operands),
        out_specs=(whole, whole),
        scratch_shapes=[vmem(shape, dtype) for shape, dtype in OPERANDS]
        + [pltpu.SemaphoreType.DMA((len(OPERANDS),))]
        + [vmem(message, jnp.int16), vmem(message, jnp.int16)]
        + [vmem((32, 2, 8, 128), jnp.int16), vmem((32, 2, 8, 128), jnp.int16)]
        + [vmem(message, jnp.int16), vmem(message, jnp.int16)]
        + [vmem(message, jnp.bfloat16), vmem(message, jnp.bfloat16)]
        + [vmem((32, 8, 1, 128), jnp.float32), vmem((32, 8, 1, 128), jnp.float32)]
        + [
            vmem(message, jnp.float32),
            vmem((8, 256, 128), jnp.float32),
            vmem((8, 256, 128), jnp.float32),
            vmem((4, 256, 256), jnp.float32),
            vmem((256, 128), jnp.float32),
            vmem((2, 3, 2, 16, 256), jnp.bfloat16),
            vmem((2, 3, 2, 16, 256), jnp.bfloat16),
            vmem((2, 4, 2, 8, 256), jnp.bfloat16),
            vmem((2, 4, 2, 8, 256), jnp.bfloat16),
            vmem((2, 2, 3, 2, 8, 256), jnp.bfloat16),
            vmem((2, 2, 3, 2, 8, 256), jnp.bfloat16),
            vmem((128, 256), jnp.float32),
            vmem((10, 2, 24, 256), jnp.float32),
            vmem((10, 144, 256), jnp.bfloat16),
            vmem((8, 320, 256), jnp.bfloat16),
            vmem((6, 288, 256), jnp.bfloat16),
            vmem((4, 320, 128), jnp.float32),
            vmem((7, 8, 16, 128), jnp.float32),
            vmem((320, 512), jnp.bfloat16),
            vmem((864, 1024), jnp.bfloat16),
            vmem((96, 896), jnp.bfloat16),
            vmem((8, 896), jnp.float32),
            pltpu.SemaphoreType.DMA((5,)),
            pltpu.SemaphoreType.DMA((5,)),
            pltpu.SemaphoreType.DMA((8,)),
            pltpu.SemaphoreType.DMA((8,)),
        ],
        compiler_params=pltpu.CompilerParams(
            collective_id=0, has_side_effects=True, vmem_limit_bytes=52 * 1024 * 1024
        ),
        name="unrolled_step",
    )(*(pltpu.with_memory_space_constraint(x, pltpu.HBM) for x in operands))


def solution(mesh):
    placed = (
        P(None, "slab", None, None),
        P(None, "coil", "slab", None, None),
        P(None, "coil", None, "slab", None),
        P(None, "slab"),
        P(),
        P(),
        P(),
    )
    return jax.shard_map(
        unrolled_step,
        mesh=mesh,
        in_specs=placed,
        out_specs=(P(None, "slab", "coil", None), P(None, "coil", None, "slab", None)),
        check_vma=False,
    )
```
